32 devices in a mesh: groups: 2 (over y), tx: 4 (over z), ty: 4 (over x, core).
Axes of the slice: x: 2, y: 2, z: 4, core: 2. Of those that a mesh axis runs over, the one named last changes fastest.
Arguments:
- object_field: float32 [4, 256, 512], P('groups', 'tx', 'ty'), parts along dimension 0, may hold values from -4 to 4
- probe_modes: float32 [4, 8, 128, 128], P('groups'), parts along dimension 0, may hold values from -3 to 3
- positions: int32 [192, 2], P(('groups', 'tx', 'ty')), parts along dimension 0, may hold values from 0 to 384, as said below
- counts: int32 [32], P(('groups', 'tx', 'ty')), parts along dimension 0, may hold values from 1 to 6, as said below
- intensity: float32 [192, 128, 128], P(('groups', 'tx', 'ty')), parts along dimension 0, may hold values from 0.5 to 20
Outputs:
- object_out: float32 [4, 256, 512], P('groups', 'tx', 'ty'), parts along dimension 0
- probe_out: float32 [4, 8, 128, 128], P('groups'), parts along dimension 0
The draws below stay inside these ranges and needn't reach their ends.
There are 2 independent parts, one for each index of `groups`. The reference program is written for one: setup_inputs(seed, part) draws one part's arguments, and reference() takes and returns one part's arrays. A program takes and returns all parts, laid end to end along the dimension named above; each array names one. Nothing has to cross between parts.
Inputs may be any that keep to these rules, and one draw needn't show every extreme that they name: `positions`: slot s belongs to tile t = s // 6, which covers object rows from (t // 4) * 64 on (64 rows) and columns from (t % 4) * 128 on (128 columns). The window of slot s, rows row to row + 127 and columns col to col + 127, lies inside the object and inside its tile widened by 64 pixels on every side. Tile t's live slots are its first counts[t] slots; the other slots are unused and their positions and intensity carry no meaning. Some tile has all 6 slots live.
All inputs are finite; a program needn't handle non-finite values.
Results may differ from the reference program's by a relative error of at most 0.0001.
Values sent between devices are 32-bit elements; how exact they have to be, the bound alone decides.
A program may use at most 64 MiB of HBM per device.

```python
import math
import jax
import jax.numpy as jnp
from jax import lax

P_SIZE = 128
MODES = 8
TH = 64
TW = 128
CAP = 6
ITERS = 2
NH = 256
NW = 512
TILES = 16
SLOTS = 96


def draw_positions(key, part):
    slot_ids = jnp.arange(SLOTS, dtype=jnp.int32)
    tile_of = slot_ids // CAP
    tiles_across = NW // TW
    row_low = tile_of // tiles_across * TH
    col_low = tile_of % tiles_across * TW
    row_center = row_low + jax.random.randint(jax.random.fold_in(key, 11), (SLOTS,), 0, TH, dtype=jnp.int32)
    col_center = col_low + jax.random.randint(jax.random.fold_in(key, 12), (SLOTS,), 0, TW, dtype=jnp.int32)
    margin = P_SIZE // 2
    row_start = jnp.clip(row_center - margin, 0, NH - P_SIZE)
    col_start = jnp.clip(col_center - margin, 0, NW - P_SIZE)
    return jnp.stack([row_start, col_start], axis=1).astype(jnp.int32)


def draw_counts(key, part):
    baseline = jax.random.randint(jax.random.fold_in(key, 21), (TILES,), 1, CAP // 2 + 1, dtype=jnp.int32)
    filled = jax.random.randint(jax.random.fold_in(key, 22), (TILES,), 0, 8, dtype=jnp.int32) == 0
    chosen = jnp.arange(TILES, dtype=jnp.int32) == jax.random.randint(jax.random.fold_in(key, 23), (), 0, TILES, dtype=jnp.int32)
    return jnp.where(filled | chosen, CAP, baseline).astype(jnp.int32)


def level_of(own_key, dims, split, smallest, largest):
    loudness = 1.0
    for dim, shards_of in split:
        heights = jax.random.uniform(jax.random.fold_in(jax.random.fold_in(own_key, 6), dim), (shards_of,), jnp.float32, smallest / len(split), largest / len(split))
        loudness = loudness * jnp.repeat(jnp.exp(heights), dims[dim] // shards_of).reshape((-1,) + (1,) * (len(dims) - 1 - dim))
    return loudness


def centred(stream_key, dims, deviation, reach, pieces=(), kind=jnp.bfloat16):
    result = deviation * jax.random.normal(stream_key, dims, jnp.float32)
    if pieces:
        result = result * level_of(stream_key, dims, pieces, -0.22, 0.18)
    return jnp.clip(result, -reach, reach).astype(kind)


def setup_inputs(seed: int = 0, part: int = 0) -> dict:
    key_of = jax.random.split(jax.random.key(seed), 6)
    part_splits = jax.random.split(jax.random.fold_in(key_of[5], part), 6)
    object_field = centred(part_splits[0], (2, NH, NW), 0.7, 4.0, ((1, 4), (2, 4)), jnp.float32)
    probe_modes = centred(part_splits[1], (2, MODES, P_SIZE, P_SIZE), 0.5, 3.0, (), jnp.float32)
    positions = draw_positions(jax.random.fold_in(jax.random.fold_in(key_of[5], part), 71), part)
    counts = draw_counts(jax.random.fold_in(jax.random.fold_in(key_of[5], part), 71), part)
    intensity = jnp.clip(jnp.exp(math.log(20.0) - 3.6888795 * jax.random.uniform(part_splits[4], (SLOTS, P_SIZE, P_SIZE), jnp.float32) ** level_of(part_splits[4], (SLOTS, P_SIZE, P_SIZE), ((0, 16),), -0.2, 0.2)), 0.5, 20.0)
    return dict(object_field=object_field, probe_modes=probe_modes, positions=positions, counts=counts, intensity=intensity)


precise = lax.Precision.HIGHEST

def tables(length):
    indices = jnp.arange(length, dtype=jnp.int32)
    phases = indices[:, None] * indices[None, :] % length
    angles = phases.astype(jnp.float32) * (2.0 * jnp.pi / length)
    normal_scale = 1.0 / jnp.sqrt(jnp.float32(length))
    return (jnp.cos(angles) * normal_scale, jnp.sin(angles) * normal_scale)

def transform(real_part, imag_part, cos_table, sin_table):
    left_r = jnp.einsum('ab,mbc->mac', cos_table, real_part, precision=precise) - jnp.einsum('ab,mbc->mac', sin_table, imag_part, precision=precise)
    left_i = jnp.einsum('ab,mbc->mac', cos_table, imag_part, precision=precise) + jnp.einsum('ab,mbc->mac', sin_table, real_part, precision=precise)
    out_r = jnp.einsum('mab,bc->mac', left_r, cos_table, precision=precise) - jnp.einsum('mab,bc->mac', left_i, sin_table, precision=precise)
    out_i = jnp.einsum('mab,bc->mac', left_i, cos_table, precision=precise) + jnp.einsum('mab,bc->mac', left_r, sin_table, precision=precise)
    return (out_r, out_i)

def exit_update(window, probes, measured, cos_table, sin_table):
    obj_r, obj_i = (window[0], window[1])
    probe_r, probe_i = (probes[0], probes[1])
    wave_r = probe_r * obj_r - probe_i * obj_i
    wave_i = probe_r * obj_i + probe_i * obj_r
    far_r, far_i = transform(wave_r, wave_i, cos_table, -sin_table)
    modelled = lax.optimization_barrier(jnp.sum(far_r * far_r + far_i * far_i, axis=0))
    factor = jnp.sqrt(measured / jnp.maximum(modelled, 1.0))
    back_r, back_i = transform(far_r * factor, far_i * factor, cos_table, sin_table)
    return (back_r - wave_r, back_i - wave_i)

def slot_terms(window, probes, lighting, change_r, change_i, weight):
    obj_r, obj_i = (window[0], window[1])
    probe_r, probe_i = (probes[0], probes[1])
    object_terms = jnp.stack([lax.optimization_barrier(jnp.sum(probe_r * change_r + probe_i * change_i, axis=0)), lax.optimization_barrier(jnp.sum(probe_r * change_i - probe_i * change_r, axis=0)), lighting]) * weight
    probe_terms = jnp.stack([obj_r * change_r + obj_i * change_i, obj_r * change_i - obj_i * change_r]) * weight
    coverage = (obj_r * obj_r + obj_i * obj_i) * weight
    return (object_terms, probe_terms, coverage)

def accumulate(object_map, probes, starts, active, intensity, cos_table, sin_table):
    length = probes.shape[-1]
    lighting = lax.optimization_barrier(jnp.sum(probes[0] * probes[0] + probes[1] * probes[1], axis=0))
    anchor_index = jnp.int32(0)

    def visit_slot(carried, element):
        totals, probe_sum, probe_weight = carried
        corner_at, weight, measured = element
        corner = (anchor_index, corner_at[0], corner_at[1])
        window = lax.dynamic_slice(object_map, corner, (2, length, length))
        change_r, change_i = exit_update(window, probes, measured, cos_table, sin_table)
        object_terms, probe_terms, coverage = slot_terms(window, probes, lighting, change_r, change_i, weight)
        region = lax.dynamic_slice(totals, corner, (3, length, length))
        totals = lax.dynamic_update_slice(totals, region + object_terms, corner)
        return ((totals, probe_sum + probe_terms, probe_weight + coverage), None)
    initial = (jnp.zeros((3,) + object_map.shape[1:], jnp.float32), jnp.zeros(probes.shape, jnp.float32), jnp.zeros((length, length), jnp.float32))
    (totals, probe_sum, probe_weight), _ = lax.scan(visit_slot, initial, (starts, active, intensity))
    return (totals, probe_sum, probe_weight)

def mixing(probes, probe_step):
    mix_r = lax.optimization_barrier(jnp.sum(probes[0] * probe_step[0] + probes[1] * probe_step[1], axis=0))
    mix_i = lax.optimization_barrier(jnp.sum(probes[0] * probe_step[1] - probes[1] * probe_step[0], axis=0))
    return (mix_r, mix_i)

def cross_term(object_map, change, starts, active, mix_r, mix_i):
    length = mix_r.shape[-1]
    anchor_index = jnp.int32(0)

    def visit_slot(running, element):
        corner_at, weight = element
        corner = (anchor_index, corner_at[0], corner_at[1])
        object_win = lax.dynamic_slice(object_map, corner, (2, length, length))
        change_win = lax.dynamic_slice(change, corner, (2, length, length))
        aligned = change_win[0] * object_win[0] + change_win[1] * object_win[1]
        rotated = change_win[0] * object_win[1] - change_win[1] * object_win[0]
        return (running + weight * jnp.sum(aligned * mix_r - rotated * mix_i), None)
    running, _ = lax.scan(visit_slot, jnp.zeros((), jnp.float32), (starts, active))
    return running

def solve_steps(object_curve, cross_curve, probe_curve, object_slope, probe_slope):
    object_diag = 1.1 * object_curve + 0.001
    probe_diag = 1.1 * probe_curve + 0.001
    determinant = object_diag * probe_diag - cross_curve * cross_curve
    object_rate = (probe_diag * object_slope - cross_curve * probe_slope) / determinant
    probe_rate = (object_diag * probe_slope - cross_curve * object_slope) / determinant
    return (object_rate, probe_rate)

def reference(object_field, probe_modes, positions, counts, intensity):
    length = probe_modes.shape[-1]
    cos_table, sin_table = tables(length)
    slot_ids = jnp.arange(positions.shape[0], dtype=jnp.int32)
    active = (slot_ids % CAP < counts[slot_ids // CAP]).astype(jnp.float32)
    object_map = object_field
    probes = probe_modes
    for repeat in range(ITERS):
        totals, probe_sum, probe_weight = accumulate(object_map, probes, positions, active, intensity, cos_table, sin_table)
        change = totals[:2] / jnp.maximum(totals[2], 1.0)
        probe_step = probe_sum / (probe_weight + 1e-05)
        object_curve = jnp.sum((change[0] * change[0] + change[1] * change[1]) * totals[2])
        object_slope = jnp.sum(totals[:2] * change)
        probe_curve = jnp.sum((probe_step[0] * probe_step[0] + probe_step[1] * probe_step[1]) * probe_weight)
        probe_slope = jnp.sum(probe_sum * probe_step)
        mix_r, mix_i = mixing(probes, probe_step)
        cross_curve = cross_term(object_map, change, positions, active, mix_r, mix_i)
        object_rate, probe_rate = solve_steps(object_curve, cross_curve, probe_curve, object_slope, probe_slope)
        object_map = object_map + object_rate * change
        probes = probes + probe_rate * probe_step
    return (object_map, probes)
```

```python
import jax
import jax.numpy as jnp
import ml_dtypes
import numpy as np
from jax import lax
from jax.experimental import pallas as pl
from jax.experimental.pallas import tpu as pltpu
from jax.sharding import PartitionSpec as P

ITERS = 2


def with_halo(value, sides, width):
    for axis, dim in sides:
        size, length = (lax.axis_size(axis), value.shape[dim])
        up = [(i, (i + 1) % size) for i in range(size - 1)]
        down = [(j, i) for i, j in up]
        last = lax.slice_in_dim(value, length - width, length, axis=dim)
        first = lax.slice_in_dim(value, 0, width, axis=dim)
        before = lax.ppermute(last, axis, up)
        after = lax.ppermute(first, axis, down)
        value = jnp.concatenate([before, value, after], axis=dim)
    return value


def from_behind(block, axis, distance):
    devices = range(lax.axis_size(axis))
    route = [(i - distance, i) for i in devices if i - distance in devices]
    return lax.ppermute(block, axis, route)


def split_tables(length):
    indices = np.arange(length)
    angles = (indices[:, None] * indices[None, :] % length) * (2.0 * np.pi / length)
    cos_table = np.cos(angles) / np.sqrt(length)
    sin_table = np.sin(angles) / np.sqrt(length)
    forward = np.block([[cos_table, sin_table], [-sin_table, cos_table]])
    inverse = np.block([[cos_table, -sin_table], [sin_table, cos_table]])

    def halves(table):
        coarse = table.astype(np.float32).astype(ml_dtypes.bfloat16)
        fine = (table - coarse.astype(np.float64)).astype(ml_dtypes.bfloat16)
        return (coarse, fine)

    lefts, rights = ([], [])
    for left, right in ((forward, inverse), (inverse, forward)):
        coarse, fine = halves(left)
        lefts.append(np.concatenate([coarse, fine, coarse], axis=1))
        coarse, fine = halves(right)
        rights.append(np.concatenate([coarse, coarse, fine], axis=0))
    return (np.stack(lefts), np.stack(rights))


def halve(value):
    coarse = value.astype(jnp.bfloat16)
    return (coarse, (value - coarse.astype(jnp.float32)).astype(jnp.bfloat16))


def multiply(left, right):
    return jnp.dot(left, right, preferred_element_type=jnp.float32)


def from_left(table, value):
    coarse, fine = halve(value)
    return multiply(table, jnp.concatenate([coarse, coarse, fine], axis=0))


def from_right(value, table):
    coarse, fine = halve(value)
    return multiply(jnp.concatenate([coarse, fine, coarse], axis=1), table)


def regroup(value, length):
    top, bottom = (value[:length], value[length:])
    return jnp.concatenate(
        [
            jnp.concatenate([top[:, :length], bottom[:, :length]], axis=1),
            jnp.concatenate([top[:, length:], bottom[:, length:]], axis=1),
        ],
        axis=0,
    )


def slots_kernel(
    starts, counts, object_map, probes, intensity, lefts, rights, totals, sums, window, far, lit
):
    modes, length = (probes.shape[1], probes.shape[-1])
    breadth = object_map.shape[-1]
    tall = length // 8
    sublane = lax.broadcasted_iota(jnp.int32, (tall, 8, length), 1)
    sublane_more = lax.broadcasted_iota(jnp.int32, (tall + 1, 8, length), 1)
    totals[...] = jnp.zeros_like(totals)
    sums[...] = jnp.zeros_like(sums)
    lighting = jnp.zeros((length, length), jnp.float32)
    for mode in range(modes):
        lighting += probes[0, mode] * probes[0, mode] + probes[1, mode] * probes[1, mode]
    lit[...] = lighting

    def visit_slot(slot, carry):
        row, col = (starts[slot, 0], starts[slot, 1])
        tile = jnp.minimum(row // 8, object_map.shape[1] - tall - 1)
        shift = row - 8 * tile
        back = lax.rem(breadth - col, breadth)
        for plane in range(2):
            wide = object_map[plane, pl.ds(tile, tall + 1)]
            wide = pltpu.roll(wide, back, 2)[:, :, :length]
            wide = pltpu.roll(wide, lax.rem(8 - shift, 8), 1)
            wide = jnp.where(sublane + shift < 8, wide[:tall], wide[1:])
            window[plane] = wide.reshape(length, length)
        modelled = jnp.zeros((length, length), jnp.float32)
        for pair in range(modes // 2):
            obj_r, obj_i = (window[0], window[1])
            waves_r, waves_i = ([], [])
            for mode in (2 * pair, 2 * pair + 1):
                waves_r.append(probes[0, mode] * obj_r - probes[1, mode] * obj_i)
                waves_i.append(probes[0, mode] * obj_i + probes[1, mode] * obj_r)
            wave = jnp.concatenate(
                [jnp.concatenate(waves_r, axis=1), jnp.concatenate(waves_i, axis=1)], axis=0
            )
            half = regroup(from_left(lefts[0], wave), length)
            spread = from_right(half, rights[0])
            far[pair] = spread
            power = spread * spread
            power = power[:, :length] + power[:, length:]
            modelled += power[:length] + power[length:]
        factor = jnp.sqrt(intensity[slot] / jnp.maximum(modelled, 1.0)) - 1.0
        factor = jnp.concatenate([factor, factor], axis=1)
        factor = jnp.concatenate([factor, factor], axis=0)
        terms_r = jnp.zeros((length, length), jnp.float32)
        terms_i = jnp.zeros((length, length), jnp.float32)
        for pair in range(modes // 2):
            half = regroup(from_right(far[pair] * factor, rights[1]), length)
            change = from_left(lefts[1], half)
            obj_r, obj_i = (window[0], window[1])
            for which in range(2):
                mode = 2 * pair + which
                lanes = slice(which * length, (which + 1) * length)
                change_r, change_i = (change[:length, lanes], change[length:, lanes])
                probe_r, probe_i = (probes[0, mode], probes[1, mode])
                terms_r += probe_r * change_r + probe_i * change_i
                terms_i += probe_r * change_i - probe_i * change_r
                sums[mode] += obj_r * change_r + obj_i * change_i
                sums[modes + mode] += obj_r * change_i - obj_i * change_r
        sums[2 * modes] += window[0] * window[0] + window[1] * window[1]
        blank = jnp.zeros((1, 8, length), jnp.float32)
        margin = jnp.zeros((tall + 1, 8, breadth - length), jnp.float32)
        for plane, terms in enumerate((terms_r, terms_i, lit[...])):
            terms = pltpu.roll(terms.reshape(tall, 8, length), lax.rem(shift, 8), 1)
            terms = jnp.where(
                sublane_more >= shift,
                jnp.concatenate([terms, blank], axis=0),
                jnp.concatenate([blank, terms], axis=0),
            )
            wide = pltpu.roll(jnp.concatenate([terms, margin], axis=2), col, 2)
            totals[plane, pl.ds(tile, tall + 1)] += wide
        return carry

    lax.fori_loop(0, counts[0], visit_slot, 0)


def accumulate(object_map, probes, starts, counts, intensity, lefts, rights):
    _, modes, length, _ = probes.shape
    _, height, breadth = object_map.shape
    memory = pl.BlockSpec(memory_space=pltpu.VMEM)
    scalars = pl.BlockSpec(memory_space=pltpu.SMEM)
    totals, sums = pl.pallas_call(
        slots_kernel,
        out_shape=(
            jax.ShapeDtypeStruct((3, height // 8, 8, breadth), jnp.float32),
            jax.ShapeDtypeStruct((2 * modes + 1, length, length), jnp.float32),
        ),
        in_specs=[scalars, scalars] + [memory] * 5,
        out_specs=(memory, memory),
        scratch_shapes=[
            pltpu.VMEM((2, length, length), jnp.float32),
            pltpu.VMEM((modes // 2, 2 * length, 2 * length), jnp.float32),
            pltpu.VMEM((length, length), jnp.float32),
        ],
        compiler_params=pltpu.CompilerParams(vmem_limit_bytes=40 * 1024 * 1024),
        name="slots",
    )(starts, counts, object_map.reshape(2, height // 8, 8, breadth), probes, intensity, lefts, rights)
    return (totals.reshape(3, height, breadth), sums)


def mixing(probes, probe_step):
    mix_r = jnp.sum(probes[0] * probe_step[0] + probes[1] * probe_step[1], axis=0)
    mix_i = jnp.sum(probes[0] * probe_step[1] - probes[1] * probe_step[0], axis=0)
    return (mix_r, mix_i)


def cross_term(object_map, change, starts, active, mix_r, mix_i):
    length = mix_r.shape[-1]
    anchor_index = jnp.int32(0)

    def cross_visit_slot(running, element):
        corner_at, weight = element
        corner = (anchor_index, corner_at[0], corner_at[1])
        object_win = lax.dynamic_slice(object_map, corner, (2, length, length))
        change_win = lax.dynamic_slice(change, corner, (2, length, length))
        aligned = change_win[0] * object_win[0] + change_win[1] * object_win[1]
        rotated = change_win[0] * object_win[1] - change_win[1] * object_win[0]
        return (running + weight * jnp.sum(aligned * mix_r - rotated * mix_i), None)

    running, _ = lax.scan(cross_visit_slot, jnp.zeros((), jnp.float32), (starts, active))
    return running


def solve_steps(object_curve, cross_curve, probe_curve, object_slope, probe_slope):
    object_diag = 1.1 * object_curve + 0.001
    probe_diag = 1.1 * probe_curve + 0.001
    determinant = object_diag * probe_diag - cross_curve * cross_curve
    object_rate = (probe_diag * object_slope - cross_curve * probe_slope) / determinant
    probe_rate = (object_diag * probe_slope - cross_curve * object_slope) / determinant
    return (object_rate, probe_rate)


def widen(planes, margin):
    return with_halo(planes, (("tx", 1), ("ty", 2)), margin)


def fold_rims(totals, margin, height, breadth):
    middle = totals[:, margin : margin + height, :]
    for direction in (1, -1):
        border = totals[:, margin + height :, :] if direction == 1 else totals[:, :margin, :]
        arrived = from_behind(border, "tx", direction)
        if direction == 1:
            middle = jnp.concatenate([middle + arrived, middle[:, margin:, :]], axis=1)
        else:
            middle = jnp.concatenate([middle[:, : height - margin, :], middle + arrived], axis=1)
    interior = middle[:, :, margin : margin + breadth]
    for direction in (1, -1):
        border = middle[:, :, margin + breadth :] if direction == 1 else middle[:, :, :margin]
        arrived = from_behind(border, "ty", direction)
        if direction == 1:
            interior = jnp.concatenate(
                [interior[:, :, :margin] + arrived, interior[:, :, margin:]], axis=2
            )
        else:
            interior = jnp.concatenate(
                [interior[:, :, : breadth - margin], interior[:, :, breadth - margin :] + arrived],
                axis=2,
            )
    return interior


def shards(object_field, probe_modes, positions, counts, intensity):
    length = probe_modes.shape[-1]
    margin = length // 2
    height = object_field.shape[1]
    breadth = object_field.shape[2]
    lefts, rights = split_tables(length)
    modes = probe_modes.shape[1]
    anchor = jnp.stack(
        [lax.axis_index("tx") * height - margin, lax.axis_index("ty") * breadth - margin]
    )
    starts = positions - anchor[None, :]
    active = (jnp.arange(positions.shape[0], dtype=jnp.int32) < counts[0]).astype(jnp.float32)
    object_map = object_field
    probes = probe_modes
    extended = widen(object_map, margin)
    for repeat in range(ITERS):
        totals, sums = accumulate(extended, probes, starts, counts, intensity, lefts, rights)
        interior = fold_rims(totals, margin, height, breadth)
        change = interior[:2] / jnp.maximum(interior[2], 1.0)
        object_part = jnp.sum((change[0] * change[0] + change[1] * change[1]) * interior[2])
        slope_part = jnp.sum(interior[:2] * change)
        wide_change = widen(change, margin)
        sums = lax.psum(sums, ("tx", "ty"))
        probe_total = sums[: 2 * modes].reshape(probes.shape)
        weight_total = sums[2 * modes]
        probe_step = probe_total / (weight_total + 1e-05)
        mix_r, mix_i = mixing(probes, probe_step)
        cross_part = cross_term(extended, wide_change, starts, active, mix_r, mix_i)
        object_curve, cross_curve, object_slope = lax.psum(
            (object_part, cross_part, slope_part), ("tx", "ty")
        )
        probe_curve = jnp.sum(
            (probe_step[0] * probe_step[0] + probe_step[1] * probe_step[1]) * weight_total
        )
        probe_slope = jnp.sum(probe_total * probe_step)
        object_rate, probe_rate = solve_steps(
            object_curve, cross_curve, probe_curve, object_slope, probe_slope
        )
        object_map = object_map + object_rate * change
        probes = probes + probe_rate * probe_step
        if repeat + 1 < ITERS:
            extended = extended + object_rate * wide_change
    return (object_map, probes)


def solution(mesh):
    return jax.shard_map(
        shards,
        mesh=mesh,
        in_specs=(
            P("groups", "tx", "ty"),
            P("groups", None, None, None),
            P(("groups", "tx", "ty"), None),
            P(("groups", "tx", "ty")),
            P(("groups", "tx", "ty"), None, None),
        ),
        out_specs=(P("groups", "tx", "ty"), P("groups", None, None, None)),
        check_vma=False,
    )
```

```python
import functools

import jax
import jax.numpy as jnp
import ml_dtypes
import numpy as np
from jax import lax
from jax.experimental import pallas as pl
from jax.experimental.pallas import tpu as pltpu
from jax.sharding import PartitionSpec as P

ITERS = 2
memory = pl.BlockSpec(memory_space=pltpu.VMEM)
scalars = pl.BlockSpec(memory_space=pltpu.SMEM)


def with_halo(value, sides, width):
    for axis, dim in sides:
        size, length = (lax.axis_size(axis), value.shape[dim])
        up = [(i, (i + 1) % size) for i in range(size - 1)]
        down = [(j, i) for i, j in up]
        last = lax.slice_in_dim(value, length - width, length, axis=dim)
        first = lax.slice_in_dim(value, 0, width, axis=dim)
        before = lax.ppermute(last, axis, up)
        after = lax.ppermute(first, axis, down)
        value = jnp.concatenate([before, value, after], axis=dim)
    return value


def from_behind(block, axis, distance):
    devices = range(lax.axis_size(axis))
    route = [(i - distance, i) for i in devices if i - distance in devices]
    return lax.ppermute(block, axis, route)


def split_tables(length):
    indices = np.arange(length)
    angles = (indices[:, None] * indices[None, :] % length) * (2.0 * np.pi / length)
    cos_table = np.cos(angles) / np.sqrt(length)
    sin_table = np.sin(angles) / np.sqrt(length)
    forward = np.block([[cos_table, sin_table], [-sin_table, cos_table]])
    inverse = np.block([[cos_table, -sin_table], [sin_table, cos_table]])

    def halves(table):
        coarse = table.astype(np.float32).astype(ml_dtypes.bfloat16)
        fine = (table - coarse.astype(np.float64)).astype(ml_dtypes.bfloat16)
        return (coarse, fine)

    lefts, rights = ([], [])
    for left, right in ((forward, inverse), (inverse, forward)):
        coarse, fine = halves(left)
        lefts.append(np.concatenate([coarse, fine, coarse], axis=1))
        coarse, fine = halves(right)
        rights.append(np.concatenate([coarse, coarse, fine], axis=0))
    return (np.stack(lefts), np.stack(rights))


def halve(value):
    coarse = value.astype(jnp.bfloat16)
    return (coarse, (value - coarse.astype(jnp.float32)).astype(jnp.bfloat16))


def multiply(left, right):
    return jnp.dot(left, right, preferred_element_type=jnp.float32)


def from_left(table, value):
    coarse, fine = halve(value)
    return multiply(table, jnp.concatenate([coarse, coarse, fine], axis=0))


def from_right(value, table):
    coarse, fine = halve(value)
    return multiply(jnp.concatenate([coarse, fine, coarse], axis=1), table)


def regroup(value, length):
    top, bottom = (value[:length], value[length:])
    return jnp.concatenate(
        [
            jnp.concatenate([top[:, :length], bottom[:, :length]], axis=1),
            jnp.concatenate([top[:, length:], bottom[:, length:]], axis=1),
        ],
        axis=0,
    )


def slots_kernel(
    lead, starts, counts, object_map, probes, intensity, lefts, rights, totals, sums, window, far, lit
):
    modes, length = (probes.shape[1], probes.shape[-1])
    breadth = object_map.shape[-1]
    tall = length // 8
    per = modes // 2
    sublane = lax.broadcasted_iota(jnp.int32, (tall, 8, length), 1)
    sublane_more = lax.broadcasted_iota(jnp.int32, (tall + 1, 8, length), 1)
    totals[...] = jnp.zeros_like(totals)
    sums[...] = jnp.zeros_like(sums)
    lighting = jnp.zeros((length, length), jnp.float32)
    for mode in range(modes):
        lighting += probes[0, mode] * probes[0, mode] + probes[1, mode] * probes[1, mode]
    lit[...] = lighting

    def visit_slot(slot, carry):
        row, col = (starts[slot, 0], starts[slot, 1])
        tile = jnp.minimum(row // 8, object_map.shape[1] - tall - 1)
        shift = row - 8 * tile
        back = lax.rem(breadth + lead - col, breadth)
        onward = lax.rem(breadth - lead + col, breadth)
        for plane in range(2):
            wide = object_map[plane, pl.ds(tile, tall + 1)]
            wide = pltpu.roll(wide, back, 2)[:, :, :length]
            wide = pltpu.roll(wide, lax.rem(8 - shift, 8), 1)
            wide = jnp.where(sublane + shift < 8, wide[:tall], wide[1:])
            window[plane] = wide.reshape(length, length)
        modelled = jnp.zeros((length, length), jnp.float32)
        for pair in range(modes // 2):
            obj_r, obj_i = (window[0], window[1])
            waves_r, waves_i = ([], [])
            for mode in (2 * pair, 2 * pair + 1):
                waves_r.append(probes[0, mode] * obj_r - probes[1, mode] * obj_i)
                waves_i.append(probes[0, mode] * obj_i + probes[1, mode] * obj_r)
            wave = jnp.concatenate(
                [jnp.concatenate(waves_r, axis=1), jnp.concatenate(waves_i, axis=1)], axis=0
            )
            half = regroup(from_left(lefts[0], wave), length)
            spread = from_right(half, rights[0])
            far[pair] = spread
            power = spread * spread
            power = power[:, :length] + power[:, length:]
            modelled += power[:length] + power[length:]
        factor = jnp.sqrt(intensity[slot] / jnp.maximum(modelled, 1.0)) - 1.0
        factor = jnp.concatenate([factor, factor], axis=1)
        factor = jnp.concatenate([factor, factor], axis=0)
        terms_r = jnp.zeros((length, length), jnp.float32)
        terms_i = jnp.zeros((length, length), jnp.float32)
        for pair in range(modes // 2):
            half = regroup(from_right(far[pair] * factor, rights[1]), length)
            change = from_left(lefts[1], half)
            obj_r, obj_i = (window[0], window[1])
            for which in range(2):
                mode = 2 * pair + which
                lanes = slice(which * length, (which + 1) * length)
                change_r, change_i = (change[:length, lanes], change[length:, lanes])
                probe_r, probe_i = (probes[0, mode], probes[1, mode])
                terms_r += probe_r * change_r + probe_i * change_i
                terms_i += probe_r * change_i - probe_i * change_r
                stream, place = (mode // per, mode % per)
                sums[stream, place] += obj_r * change_r + obj_i * change_i
                sums[stream, per + place] += obj_r * change_i - obj_i * change_r
        coverage = window[0] * window[0] + window[1] * window[1]
        sums[0, 2 * per] += coverage
        sums[1, 2 * per] += coverage
        blank = jnp.zeros((1, 8, length), jnp.float32)
        margin = jnp.zeros((tall + 1, 8, breadth - length), jnp.float32)
        for plane, terms in enumerate((terms_r, terms_i, lit[...])):
            terms = pltpu.roll(terms.reshape(tall, 8, length), lax.rem(shift, 8), 1)
            terms = jnp.where(
                sublane_more >= shift,
                jnp.concatenate([terms, blank], axis=0),
                jnp.concatenate([blank, terms], axis=0),
            )
            wide = pltpu.roll(jnp.concatenate([terms, margin], axis=2), onward, 2)
            totals[plane, pl.ds(tile, tall + 1)] += wide
        return carry

    lax.fori_loop(0, counts[0], visit_slot, 0)


def accumulate(object_map, probes, starts, counts, intensity, lefts, rights, lead):
    _, modes, length, _ = probes.shape
    return pl.pallas_call(
        functools.partial(slots_kernel, lead),
        out_shape=(
            jax.ShapeDtypeStruct((3,) + object_map.shape[1:], jnp.float32),
            jax.ShapeDtypeStruct((2, modes + 1, length, length), jnp.float32),
        ),
        in_specs=[scalars, scalars] + [memory] * 5,
        out_specs=(memory, memory),
        scratch_shapes=[
            pltpu.VMEM((2, length, length), jnp.float32),
            pltpu.VMEM((modes // 2, 2 * length, 2 * length), jnp.float32),
            pltpu.VMEM((length, length), jnp.float32),
        ],
        compiler_params=pltpu.CompilerParams(vmem_limit_bytes=40 * 1024 * 1024),
        name="slots",
    )(starts, counts, object_map, probes, intensity, lefts, rights)


def mixing(probes, probe_step):
    mix_r = jnp.sum(probes[0] * probe_step[0] + probes[1] * probe_step[1], axis=0)
    mix_i = jnp.sum(probes[0] * probe_step[1] - probes[1] * probe_step[0], axis=0)
    return (mix_r, mix_i)


def cross_term(object_map, change, starts, active, mix_r, mix_i):
    length = mix_r.shape[-1]
    anchor_index = jnp.int32(0)

    def cross_visit_slot(running, element):
        corner_at, weight = element
        corner = (anchor_index, corner_at[0], corner_at[1])
        object_win = lax.dynamic_slice(object_map, corner, (2, length, length))
        change_win = lax.dynamic_slice(change, corner, (2, length, length))
        aligned = change_win[0] * object_win[0] + change_win[1] * object_win[1]
        rotated = change_win[0] * object_win[1] - change_win[1] * object_win[0]
        return (running + weight * jnp.sum(aligned * mix_r - rotated * mix_i), None)

    running, _ = lax.scan(cross_visit_slot, jnp.zeros((), jnp.float32), (starts, active))
    return running


def solve_steps(object_curve, cross_curve, probe_curve, object_slope, probe_slope):
    object_diag = 1.1 * object_curve + 0.001
    probe_diag = 1.1 * probe_curve + 0.001
    determinant = object_diag * probe_diag - cross_curve * cross_curve
    object_rate = (probe_diag * object_slope - cross_curve * probe_slope) / determinant
    probe_rate = (object_diag * probe_slope - cross_curve * object_slope) / determinant
    return (object_rate, probe_rate)


def widen(planes, margin):
    return with_halo(planes, (("tx", 1), ("ty", 2)), margin)


def fold_rims(totals, margin, height, breadth):
    middle = totals[:, margin : margin + height, :]
    for direction in (1, -1):
        border = totals[:, margin + height :, :] if direction == 1 else totals[:, :margin, :]
        arrived = from_behind(border, "tx", direction)
        if direction == 1:
            middle = jnp.concatenate([middle + arrived, middle[:, margin:, :]], axis=1)
        else:
            middle = jnp.concatenate([middle[:, : height - margin, :], middle + arrived], axis=1)
    interior = middle[:, :, margin : margin + breadth]
    for direction in (1, -1):
        border = middle[:, :, margin + breadth :] if direction == 1 else middle[:, :, :margin]
        arrived = from_behind(border, "ty", direction)
        if direction == 1:
            interior = jnp.concatenate(
                [interior[:, :, :margin] + arrived, interior[:, :, margin:]], axis=2
            )
        else:
            interior = jnp.concatenate(
                [interior[:, :, : breadth - margin], interior[:, :, breadth - margin :] + arrived],
                axis=2,
            )
    return interior


def general(object_field, probe_modes, positions, counts, intensity):
    length = probe_modes.shape[-1]
    margin = length // 2
    height = object_field.shape[1]
    breadth = object_field.shape[2]
    lefts, rights = split_tables(length)
    modes = probe_modes.shape[1]
    anchor = jnp.stack(
        [lax.axis_index("tx") * height - margin, lax.axis_index("ty") * breadth - margin]
    )
    starts = positions - anchor[None, :]
    active = (jnp.arange(positions.shape[0], dtype=jnp.int32) < counts[0]).astype(jnp.float32)
    object_map = object_field
    probes = probe_modes
    extended = widen(object_map, margin)
    for repeat in range(ITERS):
        tiled = extended.reshape(2, -1, 8, extended.shape[-1])
        totals, sums = accumulate(tiled, probes, starts, counts, intensity, lefts, rights, 0)
        totals = totals.reshape((3,) + extended.shape[1:])
        interior = fold_rims(totals, margin, height, breadth)
        change = interior[:2] / jnp.maximum(interior[2], 1.0)
        object_part = jnp.sum((change[0] * change[0] + change[1] * change[1]) * interior[2])
        slope_part = jnp.sum(interior[:2] * change)
        wide_change = widen(change, margin)
        sums = lax.psum(sums, ("tx", "ty"))
        probe_total = sums[:, :modes].reshape(2, 2, modes // 2, length, length)
        probe_total = jnp.swapaxes(probe_total, 0, 1).reshape(probes.shape)
        weight_total = sums[0, modes]
        probe_step = probe_total / (weight_total + 1e-05)
        mix_r, mix_i = mixing(probes, probe_step)
        cross_part = cross_term(extended, wide_change, starts, active, mix_r, mix_i)
        object_curve, cross_curve, object_slope = lax.psum(
            (object_part, cross_part, slope_part), ("tx", "ty")
        )
        probe_curve = jnp.sum(
            (probe_step[0] * probe_step[0] + probe_step[1] * probe_step[1]) * weight_total
        )
        probe_slope = jnp.sum(probe_total * probe_step)
        object_rate, probe_rate = solve_steps(
            object_curve, cross_curve, probe_curve, object_slope, probe_slope
        )
        object_map = object_map + object_rate * change
        probes = probes + probe_rate * probe_step
        if repeat + 1 < ITERS:
            extended = extended + object_rate * wide_change
    return (object_map, probes)


def greet(peers):
    barrier = pltpu.get_barrier_semaphore()
    for peer in peers:
        pl.semaphore_signal(barrier, 1, device_id=peer, device_id_type=pl.DeviceIdType.MESH)
    pl.semaphore_wait(barrier, len(peers))


def everyone(row, col):
    return [
        {"tx": (row + i) % 4, "ty": (col + j) % 4} for i in range(4) for j in range(4) if i or j
    ]


AROUND = [(i, j) for i in (-1, 0, 1) for j in (-1, 0, 1) if i or j]


def around(row, col, what):
    for k, (i, j) in enumerate(AROUND):
        inside = (row + i >= 0) & (row + i < 4) & (col + j >= 0) & (col + j < 4)
        pl.when(inside)(functools.partial(what, k, i, j))


def copy_to(source, target, send, arrive, index, peer):
    return pltpu.make_async_remote_copy(
        src_ref=source,
        dst_ref=target,
        send_sem=send.at[index],
        recv_sem=arrive.at[index],
        device_id=peer,
        device_id_type=pl.DeviceIdType.MESH,
    )


def halo_copy(block, halo, send, arrive, base, row, col, k, i, j):
    opposite = AROUND.index((-i, -j))
    return pltpu.make_async_remote_copy(
        src_ref=block,
        dst_ref=halo.at[opposite],
        send_sem=send.at[base + k],
        recv_sem=arrive.at[base + opposite],
        device_id={"tx": row + i, "ty": col + j},
        device_id_type=pl.DeviceIdType.MESH,
    )


def halo_wait(block, halo, send, arrive, base, row, col, k, i, j):
    halo_copy(block, halo, send, arrive, base, row, col, k, i, j).wait_send()
    pltpu.make_async_remote_copy(
        src_ref=block,
        dst_ref=halo.at[k],
        send_sem=send.at[base + k],
        recv_sem=arrive.at[base + k],
        device_id={"tx": row + i, "ty": col + j},
        device_id_type=pl.DeviceIdType.MESH,
    ).wait_recv()


def spread_halo(own, halo, wide):
    high, broad = (own.shape[1], own.shape[-1])
    early = lax.broadcasted_iota(jnp.int32, own.shape, 3) < broad // 2
    for i in (-1, 0, 1):
        rows = slice((i + 1) * high, (i + 2) * high)
        middle = own if i == 0 else halo[AROUND.index((i, 0))]
        wide[:, rows, :, :broad] = middle
        wide[:, rows, :, broad:] = jnp.where(
            early, halo[AROUND.index((i, 1))], halo[AROUND.index((i, -1))]
        )


def widen_kernel(own, wide, halo, send, arrive):
    row, col = (lax.axis_index("tx"), lax.axis_index("ty"))
    halo[...] = jnp.zeros_like(halo)
    greet(everyone(row, col))
    common = (own, halo, send, arrive, 0, row, col)
    around(row, col, lambda k, i, j: halo_copy(*common, k, i, j).start())
    around(row, col, lambda k, i, j: halo_wait(*common, k, i, j))
    spread_halo(own[...], halo, wide)


def widen_tiles(own):
    two, high, _, broad = own.shape
    return pl.pallas_call(
        widen_kernel,
        out_shape=jax.ShapeDtypeStruct((two, 3 * high, 8, 2 * broad), jnp.float32),
        in_specs=[memory],
        out_specs=memory,
        scratch_shapes=[
            pltpu.VMEM((8,) + own.shape, jnp.float32),
            pltpu.SemaphoreType.DMA((8,)),
            pltpu.SemaphoreType.DMA((8,)),
        ],
        compiler_params=pltpu.CompilerParams(
            collective_id=0, has_side_effects=True, vmem_limit_bytes=40 * 1024 * 1024
        ),
        name="widen",
    )(own)


def in_rows(values, lanes):
    at = lax.broadcasted_iota(jnp.int32, (8, lanes), 0)
    result = jnp.zeros((8, lanes), jnp.float32)
    for place, value in enumerate(values):
        result = jnp.where(at == place, value, result)
    return result


def combine_kernel(
    totals, sums, wide, step, parts, rims, own, halo, r1, acc, ra2, acca, rb2, accb, ra3, rb3, got,
    send, arrive,
):
    row, col = (lax.axis_index("tx"), lax.axis_index("ty"))
    core, side = (col % 2, col // 2)
    planes = step.shape[1]
    high, broad = (own.shape[1], own.shape[-1])
    rims[...] = jnp.zeros_like(rims)
    halo[...] = jnp.zeros_like(halo)
    greet(everyone(row, col))
    partner = {"tx": row, "ty": side * 2 + (1 - core)}
    across = {"tx": row, "ty": (1 - side) * 2 + core}
    along = [{"tx": (row + j) % 4, "ty": col} for j in (1, 2, 3)]

    first = copy_to(sums.at[:, :, pl.ds(8 * (1 - core), 8)], r1, send, arrive, 0, partner)
    first.start()

    def rim_source(i, j):
        rows = slice((i + 1) * high, (i + 2) * high)
        lanes = slice(0, broad) if j == 0 else slice(broad, 2 * broad)
        return totals.at[:, rows, :, lanes]

    fold = (rims, send, arrive, 24, row, col)
    around(row, col, lambda k, i, j: halo_copy(rim_source(i, j), *fold, k, i, j).start())

    first.wait()
    acc[...] = sums[:, :, pl.ds(8 * core, 8)] + r1[...]
    second = [copy_to(acc.at[0, :, pl.ds(4 * (1 - side), 4)], ra2, send, arrive, 1, across)]
    for j in (1, 2, 3):
        source = acc.at[1, :, pl.ds(2 * ((row + j) % 4), 2)]
        second.append(copy_to(source, rb2.at[j - 1], send, arrive, 1 + j, along[j - 1]))
    for copy in second:
        copy.start()

    around(row, col, lambda k, i, j: halo_wait(rim_source(i, j), *fold, k, i, j))
    early = lax.broadcasted_iota(jnp.int32, (3,) + own.shape[1:], 3) < broad // 2
    interior = totals[:, high : 2 * high, :, :broad]
    for i in (-1, 1):
        interior += rims[AROUND.index((i, 0))]
    for i in (-1, 0, 1):
        interior += jnp.where(early, rims[AROUND.index((i, -1))], rims[AROUND.index((i, 1))])
    change = interior[:2] / jnp.maximum(interior[2], 1.0)
    own[...] = change
    spread = (own, halo, send, arrive, 32, row, col)
    around(row, col, lambda k, i, j: halo_copy(*spread, k, i, j).start())
    curve = jnp.sum((change[0] * change[0] + change[1] * change[1]) * interior[2])
    slope = jnp.sum(interior[:2] * change)

    for copy in second:
        copy.wait()
    acca[...] = acc[0, :, pl.ds(4 * side, 4)] + ra2[...]
    accb[...] = acc[1, :, pl.ds(2 * row, 2)] + rb2[0] + rb2[1] + rb2[2]
    third = [copy_to(accb.at[:, pl.ds(1 - side, 1)], rb3, send, arrive, 5, across)]
    for j in (1, 2, 3):
        source = acca.at[:, pl.ds((row + j) % 4, 1)]
        third.append(copy_to(source, ra3.at[j - 1], send, arrive, 5 + j, along[j - 1]))
    for copy in third:
        copy.start()
    for copy in third:
        copy.wait()
    sum_a = acca[:, pl.ds(row, 1)] + ra3[0] + ra3[1] + ra3[2]
    sum_b = accb[:, pl.ds(side, 1)] + rb3[...]
    at_a = 8 * core + 4 * side + row
    at_b = 8 * core + 2 * row + side
    probe_curve, probe_slope = (jnp.float32(0.0), jnp.float32(0.0))
    for stream, (total, at) in enumerate(((sum_a, at_a), (sum_b, at_b))):
        weight = total[planes:]
        found = total[:planes] / (weight + 1e-05)
        got[stream, :, pl.ds(at, 1)] = found
        probe_curve += jnp.sum(found * found * weight)
        probe_slope += jnp.sum(total[:planes] * found)

    def give(stream, at, count, index, peer):
        block = got.at[stream, :, pl.ds(at, count)]
        return copy_to(block, block, send, arrive, index, peer)

    fourth = [give(1, at_b, 1, 9, across)]
    for j in (1, 2, 3):
        fourth.append(give(0, at_a, 1, 9 + j, along[j - 1]))
    for copy in fourth:
        copy.start()
    for copy in fourth:
        copy.wait()
    fifth = [give(0, 8 * core + 4 * side, 4, 13, across)]
    for j in (1, 2, 3):
        fifth.append(give(1, 8 * core + 2 * row, 2, 13 + j, along[j - 1]))
    for copy in fifth:
        copy.start()
    parts[...] = in_rows((curve, slope, probe_curve, probe_slope), parts.shape[-1])
    around(row, col, lambda k, i, j: halo_wait(*spread, k, i, j))
    spread_halo(own[...], halo, wide)
    for copy in fifth:
        copy.wait()
    block = got.at[:, :, pl.ds(8 * core, 8)]
    last = copy_to(block, block, send, arrive, 17, partner)
    last.start()
    last.wait()
    step[...] = got[...]


def combine(totals, sums):
    _, rows, _, lanes = totals.shape
    planes = sums.shape[1] - 1
    length = sums.shape[-1]
    high, broad = (rows // 3, lanes // 2)
    f32 = jnp.float32
    both = planes + 1
    return pl.pallas_call(
        combine_kernel,
        out_shape=(
            jax.ShapeDtypeStruct((2, rows, 8, lanes), f32),
            jax.ShapeDtypeStruct((2, planes, 16, 8, length), f32),
            jax.ShapeDtypeStruct((8, length), f32),
        ),
        in_specs=[memory] * 2,
        out_specs=(memory,) * 3,
        scratch_shapes=[
            pltpu.VMEM((8, 3, high, 8, broad), f32),
            pltpu.VMEM((2, high, 8, broad), f32),
            pltpu.VMEM((8, 2, high, 8, broad), f32),
            pltpu.VMEM((2, both, 8, 8, length), f32),
            pltpu.VMEM((2, both, 8, 8, length), f32),
            pltpu.VMEM((both, 4, 8, length), f32),
            pltpu.VMEM((both, 4, 8, length), f32),
            pltpu.VMEM((3, both, 2, 8, length), f32),
            pltpu.VMEM((both, 2, 8, length), f32),
            pltpu.VMEM((3, both, 1, 8, length), f32),
            pltpu.VMEM((both, 1, 8, length), f32),
            pltpu.VMEM((2, planes, 16, 8, length), f32),
            pltpu.SemaphoreType.DMA((40,)),
            pltpu.SemaphoreType.DMA((40,)),
        ],
        compiler_params=pltpu.CompilerParams(
            collective_id=1, has_side_effects=True, vmem_limit_bytes=40 * 1024 * 1024
        ),
        name="combine",
    )(totals, sums.reshape(2, both, 16, 8, length))


def cross_kernel(starts, counts, object_map, change, probes, step, parts, result, product, held):
    length, modes, lanes = (probes.shape[-1], probes.shape[1], object_map.shape[-1])
    per, tall = (modes // 2, length // 8)
    lead = lanes // 4
    product[0] = change[0] * object_map[0] + change[1] * object_map[1]
    product[1] = change[0] * object_map[1] - change[1] * object_map[0]
    held[...] = jnp.zeros_like(held)
    sublane = lax.broadcasted_iota(jnp.int32, (tall, 8, length), 1)

    def visit_slot(slot, carry):
        row, col = (starts[slot, 0], starts[slot, 1])
        tile = jnp.minimum(row // 8, object_map.shape[1] - tall - 1)
        shift = row - 8 * tile
        back = lax.rem(lanes + lead - col, lanes)
        for plane in range(2):
            wide = product[plane, pl.ds(tile, tall + 1)]
            wide = pltpu.roll(wide, back, 2)[:, :, :length]
            wide = pltpu.roll(wide, lax.rem(8 - shift, 8), 1)
            held[plane] += jnp.where(sublane + shift < 8, wide[:tall], wide[1:])
        return carry

    lax.fori_loop(0, counts[0], visit_slot, 0)
    mix_r = jnp.zeros(held.shape[1:], jnp.float32)
    mix_i = jnp.zeros(held.shape[1:], jnp.float32)
    for mode in range(modes):
        stream, place = (mode // per, mode % per)
        step_r, step_i = (step[stream, place], step[stream, per + place])
        mix_r += probes[0, mode] * step_r + probes[1, mode] * step_i
        mix_i += probes[0, mode] * step_i - probes[1, mode] * step_r
    cross = jnp.sum(held[0] * mix_r - held[1] * mix_i)
    at = lax.broadcasted_iota(jnp.int32, parts.shape, 0)
    result[...] = jnp.where(at == 4, cross, parts[...])


def cross(starts, counts, object_map, change, probes, step, parts):
    return pl.pallas_call(
        cross_kernel,
        out_shape=jax.ShapeDtypeStruct(parts.shape, jnp.float32),
        in_specs=[scalars, scalars] + [memory] * 5,
        out_specs=memory,
        scratch_shapes=[
            pltpu.VMEM(object_map.shape, jnp.float32),
            pltpu.VMEM((2,) + probes.shape[2:], jnp.float32),
        ],
        compiler_params=pltpu.CompilerParams(vmem_limit_bytes=40 * 1024 * 1024),
        name="cross",
    )(starts, counts, object_map, change, probes, step, parts)


def advance_kernel(parts, object_map, change, probes, step, new_map, new_probes, inbox, send, arrive):
    row, col = (lax.axis_index("tx"), lax.axis_index("ty"))
    peers = everyone(row, col)
    greet(peers)
    copies = [
        copy_to(parts, inbox.at[k], send, arrive, k, peer) for k, peer in enumerate(peers)
    ]
    for copy in copies:
        copy.start()
    for copy in copies:
        copy.wait()
    modes = probes.shape[1]
    per = modes // 2
    total = parts[...] + jnp.sum(inbox[...], axis=0)
    object_curve, object_slope = (total[0:1], total[1:2])
    probe_curve, probe_slope = (total[2:3], total[3:4])
    object_rate, probe_rate = solve_steps(
        object_curve, total[4:5], probe_curve, object_slope, probe_slope
    )
    object_rate = jnp.broadcast_to(object_rate, (8, parts.shape[-1]))
    probe_rate = jnp.broadcast_to(probe_rate, (8, parts.shape[-1]))
    rates = jnp.concatenate([object_rate, object_rate], axis=1)
    new_map[...] = object_map[...] + rates * change[...]
    for mode in range(modes):
        stream, place = (mode // per, mode % per)
        new_probes[0, mode] = probes[0, mode] + probe_rate * step[stream, place]
        new_probes[1, mode] = probes[1, mode] + probe_rate * step[stream, per + place]


def advance(parts, object_map, change, probes, step):
    return pl.pallas_call(
        advance_kernel,
        out_shape=(
            jax.ShapeDtypeStruct(object_map.shape, jnp.float32),
            jax.ShapeDtypeStruct(probes.shape, jnp.float32),
        ),
        in_specs=[memory] * 5,
        out_specs=(memory, memory),
        scratch_shapes=[
            pltpu.VMEM((15,) + parts.shape, jnp.float32),
            pltpu.SemaphoreType.DMA((15,)),
            pltpu.SemaphoreType.DMA((15,)),
        ],
        compiler_params=pltpu.CompilerParams(
            collective_id=2, has_side_effects=True, vmem_limit_bytes=40 * 1024 * 1024
        ),
        name="advance",
    )(parts, object_map, change, probes, step)


def direct(object_field, probe_modes, positions, counts, intensity):
    two, modes, length, _ = probe_modes.shape
    margin = length // 2
    _, height, breadth = object_field.shape
    lefts, rights = split_tables(length)
    anchor = jnp.stack(
        [lax.axis_index("tx") * height - margin, lax.axis_index("ty") * breadth - margin]
    )
    starts = positions - anchor[None, :]
    object_map = widen_tiles(object_field.reshape(2, height // 8, 8, breadth))
    probes = probe_modes
    for _ in range(ITERS):
        totals, sums = accumulate(
            object_map, probes, starts, counts, intensity, lefts, rights, margin
        )
        change, step, parts = combine(totals, sums)
        tiles = probes.reshape(2, modes, length // 8, 8, length)
        parts = cross(starts, counts, object_map, change, tiles, step, parts)
        object_map, tiles = advance(parts, object_map, change, tiles, step)
        probes = tiles.reshape(probes.shape)
    own = object_map[:, height // 8 : height // 4, :, :breadth]
    return (own.reshape(object_field.shape), probes)


def shards(object_field, probe_modes, positions, counts, intensity):
    _, height, breadth = object_field.shape
    length = probe_modes.shape[-1]
    grid = (lax.axis_size("tx"), lax.axis_size("ty"))
    arguments = (object_field, probe_modes, positions, counts, intensity)
    if grid == (4, 4) and length == 128 and (2 * height, breadth) == (length, length):
        return direct(*arguments)
    return general(*arguments)


def solution(mesh):
    return jax.shard_map(
        shards,
        mesh=mesh,
        in_specs=(
            P("groups", "tx", "ty"),
            P("groups", None, None, None),
            P(("groups", "tx", "ty"), None),
            P(("groups", "tx", "ty")),
            P(("groups", "tx", "ty"), None, None),
        ),
        out_specs=(P("groups", "tx", "ty"), P("groups", None, None, None)),
        check_vma=False,
    )
```

```python
import functools

import jax
import jax.numpy as jnp
import ml_dtypes
import numpy as np
from jax import lax
from jax.experimental import pallas as pl
from jax.experimental.pallas import tpu as pltpu
from jax.sharding import PartitionSpec as P

ITERS = 2
memory = pl.BlockSpec(memory_space=pltpu.VMEM)
scalars = pl.BlockSpec(memory_space=pltpu.SMEM)


def with_halo(value, sides, width):
    for axis, dim in sides:
        size, length = (lax.axis_size(axis), value.shape[dim])
        up = [(i, (i + 1) % size) for i in range(size - 1)]
        down = [(j, i) for i, j in up]
        last = lax.slice_in_dim(value, length - width, length, axis=dim)
        first = lax.slice_in_dim(value, 0, width, axis=dim)
        before = lax.ppermute(last, axis, up)
        after = lax.ppermute(first, axis, down)
        value = jnp.concatenate([before, value, after], axis=dim)
    return value


def from_behind(block, axis, distance):
    devices = range(lax.axis_size(axis))
    route = [(i - distance, i) for i in devices if i - distance in devices]
    return lax.ppermute(block, axis, route)


def split_tables(length):
    indices = np.arange(length)
    angles = (indices[:, None] * indices[None, :] % length) * (2.0 * np.pi / length)
    cos_table = np.cos(angles) / np.sqrt(length)
    sin_table = np.sin(angles) / np.sqrt(length)
    forward = np.block([[cos_table, sin_table], [-sin_table, cos_table]])
    inverse = np.block([[cos_table, -sin_table], [sin_table, cos_table]])

    def halves(table):
        coarse = table.astype(np.float32).astype(ml_dtypes.bfloat16)
        fine = (table - coarse.astype(np.float64)).astype(ml_dtypes.bfloat16)
        return (coarse, fine)

    lefts, rights = ([], [])
    for left, right in ((forward, inverse), (inverse, forward)):
        coarse, fine = halves(left)
        lefts.append(np.concatenate([coarse, fine, coarse], axis=1))
        coarse, fine = halves(right)
        rights.append(np.concatenate([coarse, coarse, fine], axis=0))
    return (np.stack(lefts), np.stack(rights))


def halve(value):
    coarse = value.astype(jnp.bfloat16)
    return (coarse, (value - coarse.astype(jnp.float32)).astype(jnp.bfloat16))


def multiply(left, right):
    return jnp.dot(left, right, preferred_element_type=jnp.float32)


def from_left(table, value):
    coarse, fine = halve(value)
    return multiply(table, jnp.concatenate([coarse, coarse, fine], axis=0))


def from_right(value, table):
    coarse, fine = halve(value)
    return multiply(jnp.concatenate([coarse, fine, coarse], axis=1), table)


def regroup(value, length):
    top, bottom = (value[:length], value[length:])
    return jnp.concatenate(
        [
            jnp.concatenate([top[:, :length], bottom[:, :length]], axis=1),
            jnp.concatenate([top[:, length:], bottom[:, length:]], axis=1),
        ],
        axis=0,
    )


def slots_kernel(
    lead, starts, counts, object_map, probes, intensity, lefts, rights, totals, sums, window, far, lit
):
    modes, length = (probes.shape[1], probes.shape[-1])
    breadth = object_map.shape[-1]
    tall = length // 8
    per = modes // 2
    sublane = lax.broadcasted_iota(jnp.int32, (tall, 8, length), 1)
    sublane_more = lax.broadcasted_iota(jnp.int32, (tall + 1, 8, length), 1)
    totals[...] = jnp.zeros_like(totals)
    sums[...] = jnp.zeros_like(sums)
    lighting = jnp.zeros((length, length), jnp.float32)
    for mode in range(modes):
        lighting += probes[0, mode] * probes[0, mode] + probes[1, mode] * probes[1, mode]
    lit[...] = lighting

    def visit_slot(slot, carry):
        row, col = (starts[slot, 0], starts[slot, 1])
        tile = jnp.minimum(row // 8, object_map.shape[1] - tall - 1)
        shift = row - 8 * tile
        back = lax.rem(breadth + lead - col, breadth)
        onward = lax.rem(breadth - lead + col, breadth)
        for plane in range(2):
            wide = object_map[plane, pl.ds(tile, tall + 1)]
            wide = pltpu.roll(wide, back, 2)[:, :, :length]
            wide = pltpu.roll(wide, lax.rem(8 - shift, 8), 1)
            wide = jnp.where(sublane + shift < 8, wide[:tall], wide[1:])
            window[plane] = wide.reshape(length, length)
        modelled = jnp.zeros((length, length), jnp.float32)
        for pair in range(modes // 2):
            obj_r, obj_i = (window[0], window[1])
            waves_r, waves_i = ([], [])
            for mode in (2 * pair, 2 * pair + 1):
                waves_r.append(probes[0, mode] * obj_r - probes[1, mode] * obj_i)
                waves_i.append(probes[0, mode] * obj_i + probes[1, mode] * obj_r)
            wave = jnp.concatenate(
                [jnp.concatenate(waves_r, axis=1), jnp.concatenate(waves_i, axis=1)], axis=0
            )
            half = regroup(from_left(lefts[0], wave), length)
            spread = from_right(half, rights[0])
            far[pair] = spread
            power = spread * spread
            power = power[:, :length] + power[:, length:]
            modelled += power[:length] + power[length:]
        factor = jnp.sqrt(intensity[slot] / jnp.maximum(modelled, 1.0)) - 1.0
        factor = jnp.concatenate([factor, factor], axis=1)
        factor = jnp.concatenate([factor, factor], axis=0)
        terms_r = jnp.zeros((length, length), jnp.float32)
        terms_i = jnp.zeros((length, length), jnp.float32)
        for pair in range(modes // 2):
            half = regroup(from_right(far[pair] * factor, rights[1]), length)
            change = from_left(lefts[1], half)
            obj_r, obj_i = (window[0], window[1])
            for which in range(2):
                mode = 2 * pair + which
                lanes = slice(which * length, (which + 1) * length)
                change_r, change_i = (change[:length, lanes], change[length:, lanes])
                probe_r, probe_i = (probes[0, mode], probes[1, mode])
                terms_r += probe_r * change_r + probe_i * change_i
                terms_i += probe_r * change_i - probe_i * change_r
                stream, place = (mode // per, mode % per)
                sums[stream, place] += obj_r * change_r + obj_i * change_i
                sums[stream, per + place] += obj_r * change_i - obj_i * change_r
        coverage = window[0] * window[0] + window[1] * window[1]
        sums[0, 2 * per] += coverage
        sums[1, 2 * per] += coverage
        blank = jnp.zeros((1, 8, length), jnp.float32)
        margin = jnp.zeros((tall + 1, 8, breadth - length), jnp.float32)
        for plane, terms in enumerate((terms_r, terms_i, lit[...])):
            terms = pltpu.roll(terms.reshape(tall, 8, length), lax.rem(shift, 8), 1)
            terms = jnp.where(
                sublane_more >= shift,
                jnp.concatenate([terms, blank], axis=0),
                jnp.concatenate([blank, terms], axis=0),
            )
            wide = pltpu.roll(jnp.concatenate([terms, margin], axis=2), onward, 2)
            totals[plane, pl.ds(tile, tall + 1)] += wide
        return carry

    lax.fori_loop(0, counts[0], visit_slot, 0)


def accumulate(object_map, probes, starts, counts, intensity, lefts, rights, lead):
    _, modes, length, _ = probes.shape
    return pl.pallas_call(
        functools.partial(slots_kernel, lead),
        out_shape=(
            jax.ShapeDtypeStruct((3,) + object_map.shape[1:], jnp.float32),
            jax.ShapeDtypeStruct((2, modes + 1, length, length), jnp.float32),
        ),
        in_specs=[scalars, scalars] + [memory] * 5,
        out_specs=(memory, memory),
        scratch_shapes=[
            pltpu.VMEM((2, length, length), jnp.float32),
            pltpu.VMEM((modes // 2, 2 * length, 2 * length), jnp.float32),
            pltpu.VMEM((length, length), jnp.float32),
        ],
        compiler_params=pltpu.CompilerParams(vmem_limit_bytes=40 * 1024 * 1024),
        name="slots",
    )(starts, counts, object_map, probes, intensity, lefts, rights)


def mixing(probes, probe_step):
    mix_r = jnp.sum(probes[0] * probe_step[0] + probes[1] * probe_step[1], axis=0)
    mix_i = jnp.sum(probes[0] * probe_step[1] - probes[1] * probe_step[0], axis=0)
    return (mix_r, mix_i)


def cross_term(object_map, change, starts, active, mix_r, mix_i):
    length = mix_r.shape[-1]
    anchor_index = jnp.int32(0)

    def cross_visit_slot(running, element):
        corner_at, weight = element
        corner = (anchor_index, corner_at[0], corner_at[1])
        object_win = lax.dynamic_slice(object_map, corner, (2, length, length))
        change_win = lax.dynamic_slice(change, corner, (2, length, length))
        aligned = change_win[0] * object_win[0] + change_win[1] * object_win[1]
        rotated = change_win[0] * object_win[1] - change_win[1] * object_win[0]
        return (running + weight * jnp.sum(aligned * mix_r - rotated * mix_i), None)

    running, _ = lax.scan(cross_visit_slot, jnp.zeros((), jnp.float32), (starts, active))
    return running


def solve_steps(object_curve, cross_curve, probe_curve, object_slope, probe_slope):
    object_diag = 1.1 * object_curve + 0.001
    probe_diag = 1.1 * probe_curve + 0.001
    determinant = object_diag * probe_diag - cross_curve * cross_curve
    object_rate = (probe_diag * object_slope - cross_curve * probe_slope) / determinant
    probe_rate = (object_diag * probe_slope - cross_curve * object_slope) / determinant
    return (object_rate, probe_rate)


def widen(planes, margin):
    return with_halo(planes, (("tx", 1), ("ty", 2)), margin)


def fold_rims(totals, margin, height, breadth):
    middle = totals[:, margin : margin + height, :]
    for direction in (1, -1):
        border = totals[:, margin + height :, :] if direction == 1 else totals[:, :margin, :]
        arrived = from_behind(border, "tx", direction)
        if direction == 1:
            middle = jnp.concatenate([middle + arrived, middle[:, margin:, :]], axis=1)
        else:
            middle = jnp.concatenate([middle[:, : height - margin, :], middle + arrived], axis=1)
    interior = middle[:, :, margin : margin + breadth]
    for direction in (1, -1):
        border = middle[:, :, margin + breadth :] if direction == 1 else middle[:, :, :margin]
        arrived = from_behind(border, "ty", direction)
        if direction == 1:
            interior = jnp.concatenate(
                [interior[:, :, :margin] + arrived, interior[:, :, margin:]], axis=2
            )
        else:
            interior = jnp.concatenate(
                [interior[:, :, : breadth - margin], interior[:, :, breadth - margin :] + arrived],
                axis=2,
            )
    return interior


def general(object_field, probe_modes, positions, counts, intensity):
    length = probe_modes.shape[-1]
    margin = length // 2
    height = object_field.shape[1]
    breadth = object_field.shape[2]
    lefts, rights = split_tables(length)
    modes = probe_modes.shape[1]
    anchor = jnp.stack(
        [lax.axis_index("tx") * height - margin, lax.axis_index("ty") * breadth - margin]
    )
    starts = positions - anchor[None, :]
    active = (jnp.arange(positions.shape[0], dtype=jnp.int32) < counts[0]).astype(jnp.float32)
    object_map = object_field
    probes = probe_modes
    extended = widen(object_map, margin)
    for repeat in range(ITERS):
        tiled = extended.reshape(2, -1, 8, extended.shape[-1])
        totals, sums = accumulate(tiled, probes, starts, counts, intensity, lefts, rights, 0)
        totals = totals.reshape((3,) + extended.shape[1:])
        interior = fold_rims(totals, margin, height, breadth)
        change = interior[:2] / jnp.maximum(interior[2], 1.0)
        object_part = jnp.sum((change[0] * change[0] + change[1] * change[1]) * interior[2])
        slope_part = jnp.sum(interior[:2] * change)
        wide_change = widen(change, margin)
        sums = lax.psum(sums, ("tx", "ty"))
        probe_total = sums[:, :modes].reshape(2, 2, modes // 2, length, length)
        probe_total = jnp.swapaxes(probe_total, 0, 1).reshape(probes.shape)
        weight_total = sums[0, modes]
        probe_step = probe_total / (weight_total + 1e-05)
        mix_r, mix_i = mixing(probes, probe_step)
        cross_part = cross_term(extended, wide_change, starts, active, mix_r, mix_i)
        object_curve, cross_curve, object_slope = lax.psum(
            (object_part, cross_part, slope_part), ("tx", "ty")
        )
        probe_curve = jnp.sum(
            (probe_step[0] * probe_step[0] + probe_step[1] * probe_step[1]) * weight_total
        )
        probe_slope = jnp.sum(probe_total * probe_step)
        object_rate, probe_rate = solve_steps(
            object_curve, cross_curve, probe_curve, object_slope, probe_slope
        )
        object_map = object_map + object_rate * change
        probes = probes + probe_rate * probe_step
        if repeat + 1 < ITERS:
            extended = extended + object_rate * wide_change
    return (object_map, probes)


def greet(peers):
    barrier = pltpu.get_barrier_semaphore()
    for peer in peers:
        pl.semaphore_signal(barrier, 1, device_id=peer, device_id_type=pl.DeviceIdType.MESH)
    pl.semaphore_wait(barrier, len(peers))


def everyone(row, col):
    return [
        {"tx": (row + i) % 4, "ty": (col + j) % 4} for i in range(4) for j in range(4) if i or j
    ]


AROUND = [(i, j) for i in (-1, 0, 1) for j in (-1, 0, 1) if i or j]


def around(row, col, what):
    for k, (i, j) in enumerate(AROUND):
        inside = (row + i >= 0) & (row + i < 4) & (col + j >= 0) & (col + j < 4)
        pl.when(inside)(functools.partial(what, k, i, j))


def copy_to(source, target, send, arrive, index, peer):
    return pltpu.make_async_remote_copy(
        src_ref=source,
        dst_ref=target,
        send_sem=send.at[index],
        recv_sem=arrive.at[index],
        device_id=peer,
        device_id_type=pl.DeviceIdType.MESH,
    )


def halo_copy(block, halo, send, arrive, base, row, col, k, i, j):
    opposite = AROUND.index((-i, -j))
    return pltpu.make_async_remote_copy(
        src_ref=block,
        dst_ref=halo.at[opposite],
        send_sem=send.at[base + k],
        recv_sem=arrive.at[base + opposite],
        device_id={"tx": row + i, "ty": col + j},
        device_id_type=pl.DeviceIdType.MESH,
    )


def halo_wait(block, halo, send, arrive, base, row, col, k, i, j):
    halo_copy(block, halo, send, arrive, base, row, col, k, i, j).wait_send()
    pltpu.make_async_remote_copy(
        src_ref=block,
        dst_ref=halo.at[k],
        send_sem=send.at[base + k],
        recv_sem=arrive.at[base + k],
        device_id={"tx": row + i, "ty": col + j},
        device_id_type=pl.DeviceIdType.MESH,
    ).wait_recv()


def spread_halo(own, halo, wide):
    high, broad = (own.shape[1], own.shape[-1])
    early = lax.broadcasted_iota(jnp.int32, own.shape, 3) < broad // 2
    for i in (-1, 0, 1):
        rows = slice((i + 1) * high, (i + 2) * high)
        middle = own if i == 0 else halo[AROUND.index((i, 0))]
        wide[:, rows, :, :broad] = middle
        wide[:, rows, :, broad:] = jnp.where(
            early, halo[AROUND.index((i, 1))], halo[AROUND.index((i, -1))]
        )


def widen_kernel(own, wide, halo, send, arrive):
    row, col = (lax.axis_index("tx"), lax.axis_index("ty"))
    halo[...] = jnp.zeros_like(halo)
    greet(everyone(row, col))
    common = (own, halo, send, arrive, 0, row, col)
    around(row, col, lambda k, i, j: halo_copy(*common, k, i, j).start())
    around(row, col, lambda k, i, j: halo_wait(*common, k, i, j))
    spread_halo(own[...], halo, wide)


def widen_tiles(own):
    two, high, _, broad = own.shape
    return pl.pallas_call(
        widen_kernel,
        out_shape=jax.ShapeDtypeStruct((two, 3 * high, 8, 2 * broad), jnp.float32),
        in_specs=[memory],
        out_specs=memory,
        scratch_shapes=[
            pltpu.VMEM((8,) + own.shape, jnp.float32),
            pltpu.SemaphoreType.DMA((8,)),
            pltpu.SemaphoreType.DMA((8,)),
        ],
        compiler_params=pltpu.CompilerParams(
            collective_id=0, has_side_effects=True, vmem_limit_bytes=40 * 1024 * 1024
        ),
        name="widen",
    )(own)


def in_rows(values, lanes):
    at = lax.broadcasted_iota(jnp.int32, (8, lanes), 0)
    result = jnp.zeros((8, lanes), jnp.float32)
    for place, value in enumerate(values):
        result = jnp.where(at == place, value, result)
    return result


class Edges:
    def __init__(self, axis, source, target, base):
        self.axis, self.source, self.target, self.base = (axis, source, target, base)

    def each(self, what):
        here = lax.axis_index(self.axis)
        for k, ahead in ((0, -1), (1, 1)):
            peer = {"tx": lax.axis_index("tx"), "ty": lax.axis_index("ty")}
            peer[self.axis] = here + ahead
            pl.when((here + ahead >= 0) & (here + ahead < 4))(functools.partial(what, k, peer))

    def copy(self, k, landing, peer, send, arrive):
        return pltpu.make_async_remote_copy(
            src_ref=self.source(k),
            dst_ref=self.target(landing),
            send_sem=send.at[self.base + k],
            recv_sem=arrive.at[self.base + landing],
            device_id=peer,
            device_id_type=pl.DeviceIdType.MESH,
        )

    def start(self, send, arrive):
        self.each(lambda k, peer: self.copy(k, 1 - k, peer, send, arrive).start())

    def wait(self, send, arrive):
        def finish(k, peer):
            self.copy(k, 1 - k, peer, send, arrive).wait_send()
            self.copy(k, k, peer, send, arrive).wait_recv()

        self.each(finish)


def combine_kernel(
    totals, sums, wide, step, parts, beside, tall, over, column, near, r1, acc, ra2, acca, rb2, accb, ra3, rb3, got,
    send, arrive,
):
    row, col = (lax.axis_index("tx"), lax.axis_index("ty"))
    core, side = (col % 2, col // 2)
    planes = step.shape[1]
    high, broad = (over.shape[2], over.shape[-1])
    ends = (slice(0, high), slice(2 * high, 3 * high))
    middle = slice(high, 2 * high)
    for buffer in (beside, over, column, near):
        buffer[...] = jnp.zeros_like(buffer)
    greet(everyone(row, col))
    partner = {"tx": row, "ty": side * 2 + (1 - core)}
    across = {"tx": row, "ty": (1 - side) * 2 + core}
    along = [{"tx": (row + j) % 4, "ty": col} for j in (1, 2, 3)]

    first = copy_to(sums.at[:, :, pl.ds(8 * (1 - core), 8)], r1, send, arrive, 0, partner)
    first.start()

    broad_lanes = slice(broad, 2 * broad)
    fold_side = Edges("ty", lambda k: totals.at[:, :, :, broad_lanes], lambda k: beside.at[k], 24)
    fold_over = Edges("tx", lambda k: tall.at[:, ends[k]], lambda k: over.at[k], 26)
    halo_over = Edges("tx", lambda k: column.at[:, middle], lambda k: column.at[:, ends[k]], 28)
    halo_side = Edges("ty", lambda k: column, lambda k: near.at[k], 30)
    fold_side.start(send, arrive)

    first.wait()
    acc[...] = sums[:, :, pl.ds(8 * core, 8)] + r1[...]
    second = [copy_to(acc.at[0, :, pl.ds(4 * (1 - side), 4)], ra2, send, arrive, 1, across)]
    for j in (1, 2, 3):
        source = acc.at[1, :, pl.ds(2 * ((row + j) % 4), 2)]
        second.append(copy_to(source, rb2.at[j - 1], send, arrive, 1 + j, along[j - 1]))
    for copy in second:
        copy.start()

    fold_side.wait(send, arrive)
    early = lax.broadcasted_iota(jnp.int32, tall.shape, 3) < broad // 2
    tall[...] = totals[:, :, :, :broad] + jnp.where(early, beside[0], beside[1])
    fold_over.start(send, arrive)

    for copy in second:
        copy.wait()
    acca[...] = acc[0, :, pl.ds(4 * side, 4)] + ra2[...]
    accb[...] = acc[1, :, pl.ds(2 * row, 2)] + rb2[0] + rb2[1] + rb2[2]
    third = [copy_to(accb.at[:, pl.ds(1 - side, 1)], rb3, send, arrive, 5, across)]
    for j in (1, 2, 3):
        source = acca.at[:, pl.ds((row + j) % 4, 1)]
        third.append(copy_to(source, ra3.at[j - 1], send, arrive, 5 + j, along[j - 1]))
    for copy in third:
        copy.start()
    fold_over.wait(send, arrive)
    interior = tall[:, middle] + over[0] + over[1]
    change = interior[:2] / jnp.maximum(interior[2], 1.0)
    column[:, middle] = change
    halo_over.start(send, arrive)
    curve = jnp.sum((change[0] * change[0] + change[1] * change[1]) * interior[2])
    slope = jnp.sum(interior[:2] * change)
    for copy in third:
        copy.wait()
    sum_a = acca[:, pl.ds(row, 1)] + ra3[0] + ra3[1] + ra3[2]
    sum_b = accb[:, pl.ds(side, 1)] + rb3[...]
    at_a = 8 * core + 4 * side + row
    at_b = 8 * core + 2 * row + side
    probe_curve, probe_slope = (jnp.float32(0.0), jnp.float32(0.0))
    for stream, (total, at) in enumerate(((sum_a, at_a), (sum_b, at_b))):
        weight = total[planes:]
        found = total[:planes] / (weight + 1e-05)
        got[stream, :, pl.ds(at, 1)] = found
        probe_curve += jnp.sum(found * found * weight)
        probe_slope += jnp.sum(total[:planes] * found)

    def give(stream, at, count, index, peer):
        block = got.at[stream, :, pl.ds(at, count)]
        return copy_to(block, block, send, arrive, index, peer)

    fourth = [give(1, at_b, 1, 9, across)]
    for j in (1, 2, 3):
        fourth.append(give(0, at_a, 1, 9 + j, along[j - 1]))
    for copy in fourth:
        copy.start()
    halo_over.wait(send, arrive)
    halo_side.start(send, arrive)
    for copy in fourth:
        copy.wait()
    fifth = [give(0, 8 * core + 4 * side, 4, 13, across)]
    for j in (1, 2, 3):
        fifth.append(give(1, 8 * core + 2 * row, 2, 13 + j, along[j - 1]))
    for copy in fifth:
        copy.start()
    parts[...] = in_rows((curve, slope, probe_curve, probe_slope), parts.shape[-1])
    halo_side.wait(send, arrive)
    wide[:, :, :, :broad] = column[...]
    wide[:, :, :, broad:] = jnp.where(early[:2], near[1], near[0])
    for copy in fifth:
        copy.wait()
    block = got.at[:, :, pl.ds(8 * core, 8)]
    last = copy_to(block, block, send, arrive, 17, partner)
    last.start()
    last.wait()
    step[...] = got[...]


def combine(totals, sums):
    _, rows, _, lanes = totals.shape
    planes = sums.shape[1] - 1
    length = sums.shape[-1]
    high, broad = (rows // 3, lanes // 2)
    f32 = jnp.float32
    both = planes + 1
    return pl.pallas_call(
        combine_kernel,
        out_shape=(
            jax.ShapeDtypeStruct((2, rows, 8, lanes), f32),
            jax.ShapeDtypeStruct((2, planes, 16, 8, length), f32),
            jax.ShapeDtypeStruct((8, length), f32),
        ),
        in_specs=[memory] * 2,
        out_specs=(memory,) * 3,
        scratch_shapes=[
            pltpu.VMEM((2, 3, rows, 8, broad), f32),
            pltpu.VMEM((3, rows, 8, broad), f32),
            pltpu.VMEM((2, 3, high, 8, broad), f32),
            pltpu.VMEM((2, rows, 8, broad), f32),
            pltpu.VMEM((2, 2, rows, 8, broad), f32),
            pltpu.VMEM((2, both, 8, 8, length), f32),
            pltpu.VMEM((2, both, 8, 8, length), f32),
            pltpu.VMEM((both, 4, 8, length), f32),
            pltpu.VMEM((both, 4, 8, length), f32),
            pltpu.VMEM((3, both, 2, 8, length), f32),
            pltpu.VMEM((both, 2, 8, length), f32),
            pltpu.VMEM((3, both, 1, 8, length), f32),
            pltpu.VMEM((both, 1, 8, length), f32),
            pltpu.VMEM((2, planes, 16, 8, length), f32),
            pltpu.SemaphoreType.DMA((40,)),
            pltpu.SemaphoreType.DMA((40,)),
        ],
        compiler_params=pltpu.CompilerParams(
            collective_id=1, has_side_effects=True, vmem_limit_bytes=40 * 1024 * 1024
        ),
        name="combine",
    )(totals, sums.reshape(2, both, 16, 8, length))


def cross_kernel(starts, counts, object_map, change, probes, step, parts, result, product, held):
    length, modes, lanes = (probes.shape[-1], probes.shape[1], object_map.shape[-1])
    per, tall = (modes // 2, length // 8)
    lead = lanes // 4
    product[0] = change[0] * object_map[0] + change[1] * object_map[1]
    product[1] = change[0] * object_map[1] - change[1] * object_map[0]
    held[...] = jnp.zeros_like(held)
    sublane = lax.broadcasted_iota(jnp.int32, (tall, 8, length), 1)

    def visit_slot(slot, carry):
        row, col = (starts[slot, 0], starts[slot, 1])
        tile = jnp.minimum(row // 8, object_map.shape[1] - tall - 1)
        shift = row - 8 * tile
        back = lax.rem(lanes + lead - col, lanes)
        for plane in range(2):
            wide = product[plane, pl.ds(tile, tall + 1)]
            wide = pltpu.roll(wide, back, 2)[:, :, :length]
            wide = pltpu.roll(wide, lax.rem(8 - shift, 8), 1)
            held[plane] += jnp.where(sublane + shift < 8, wide[:tall], wide[1:])
        return carry

    lax.fori_loop(0, counts[0], visit_slot, 0)
    mix_r = jnp.zeros(held.shape[1:], jnp.float32)
    mix_i = jnp.zeros(held.shape[1:], jnp.float32)
    for mode in range(modes):
        stream, place = (mode // per, mode % per)
        step_r, step_i = (step[stream, place], step[stream, per + place])
        mix_r += probes[0, mode] * step_r + probes[1, mode] * step_i
        mix_i += probes[0, mode] * step_i - probes[1, mode] * step_r
    cross = jnp.sum(held[0] * mix_r - held[1] * mix_i)
    at = lax.broadcasted_iota(jnp.int32, parts.shape, 0)
    result[...] = jnp.where(at == 4, cross, parts[...])


def cross(starts, counts, object_map, change, probes, step, parts):
    return pl.pallas_call(
        cross_kernel,
        out_shape=jax.ShapeDtypeStruct(parts.shape, jnp.float32),
        in_specs=[scalars, scalars] + [memory] * 5,
        out_specs=memory,
        scratch_shapes=[
            pltpu.VMEM(object_map.shape, jnp.float32),
            pltpu.VMEM((2,) + probes.shape[2:], jnp.float32),
        ],
        compiler_params=pltpu.CompilerParams(vmem_limit_bytes=40 * 1024 * 1024),
        name="cross",
    )(starts, counts, object_map, change, probes, step, parts)


def advance_kernel(parts, object_map, change, probes, step, new_map, new_probes, inbox, send, arrive):
    row, col = (lax.axis_index("tx"), lax.axis_index("ty"))
    peers = everyone(row, col)
    greet(peers)
    copies = [
        copy_to(parts, inbox.at[k], send, arrive, k, peer) for k, peer in enumerate(peers)
    ]
    for copy in copies:
        copy.start()
    for copy in copies:
        copy.wait()
    modes = probes.shape[1]
    per = modes // 2
    total = parts[...] + jnp.sum(inbox[...], axis=0)
    object_curve, object_slope = (total[0:1], total[1:2])
    probe_curve, probe_slope = (total[2:3], total[3:4])
    object_rate, probe_rate = solve_steps(
        object_curve, total[4:5], probe_curve, object_slope, probe_slope
    )
    object_rate = jnp.broadcast_to(object_rate, (8, parts.shape[-1]))
    probe_rate = jnp.broadcast_to(probe_rate, (8, parts.shape[-1]))
    rates = jnp.concatenate([object_rate, object_rate], axis=1)
    new_map[...] = object_map[...] + rates * change[...]
    for mode in range(modes):
        stream, place = (mode // per, mode % per)
        new_probes[0, mode] = probes[0, mode] + probe_rate * step[stream, place]
        new_probes[1, mode] = probes[1, mode] + probe_rate * step[stream, per + place]


def advance(parts, object_map, change, probes, step):
    return pl.pallas_call(
        advance_kernel,
        out_shape=(
            jax.ShapeDtypeStruct(object_map.shape, jnp.float32),
            jax.ShapeDtypeStruct(probes.shape, jnp.float32),
        ),
        in_specs=[memory] * 5,
        out_specs=(memory, memory),
        scratch_shapes=[
            pltpu.VMEM((15,) + parts.shape, jnp.float32),
            pltpu.SemaphoreType.DMA((15,)),
            pltpu.SemaphoreType.DMA((15,)),
        ],
        compiler_params=pltpu.CompilerParams(
            collective_id=2, has_side_effects=True, vmem_limit_bytes=40 * 1024 * 1024
        ),
        name="advance",
    )(parts, object_map, change, probes, step)


def direct(object_field, probe_modes, positions, counts, intensity):
    two, modes, length, _ = probe_modes.shape
    margin = length // 2
    _, height, breadth = object_field.shape
    lefts, rights = split_tables(length)
    anchor = jnp.stack(
        [lax.axis_index("tx") * height - margin, lax.axis_index("ty") * breadth - margin]
    )
    starts = positions - anchor[None, :]
    object_map = widen_tiles(object_field.reshape(2, height // 8, 8, breadth))
    probes = probe_modes
    for _ in range(ITERS):
        totals, sums = accumulate(
            object_map, probes, starts, counts, intensity, lefts, rights, margin
        )
        change, step, parts = combine(totals, sums)
        tiles = probes.reshape(2, modes, length // 8, 8, length)
        parts = cross(starts, counts, object_map, change, tiles, step, parts)
        object_map, tiles = advance(parts, object_map, change, tiles, step)
        probes = tiles.reshape(probes.shape)
    own = object_map[:, height // 8 : height // 4, :, :breadth]
    return (own.reshape(object_field.shape), probes)


def shards(object_field, probe_modes, positions, counts, intensity):
    _, height, breadth = object_field.shape
    length = probe_modes.shape[-1]
    grid = (lax.axis_size("tx"), lax.axis_size("ty"))
    arguments = (object_field, probe_modes, positions, counts, intensity)
    if grid == (4, 4) and length == 128 and (2 * height, breadth) == (length, length):
        return direct(*arguments)
    return general(*arguments)


def solution(mesh):
    return jax.shard_map(
        shards,
        mesh=mesh,
        in_specs=(
            P("groups", "tx", "ty"),
            P("groups", None, None, None),
            P(("groups", "tx", "ty"), None),
            P(("groups", "tx", "ty")),
            P(("groups", "tx", "ty"), None, None),
        ),
        out_specs=(P("groups", "tx", "ty"), P("groups", None, None, None)),
        check_vma=False,
    )
```

```python
import functools

import jax
import jax.numpy as jnp
import ml_dtypes
import numpy as np
from jax import lax
from jax.experimental import pallas as pl
from jax.experimental.pallas import tpu as pltpu
from jax.sharding import PartitionSpec as P

ITERS = 2
memory = pl.BlockSpec(memory_space=pltpu.VMEM)
scalars = pl.BlockSpec(memory_space=pltpu.SMEM)


def with_halo(value, sides, width):
    for axis, dim in sides:
        size, length = (lax.axis_size(axis), value.shape[dim])
        up = [(i, (i + 1) % size) for i in range(size - 1)]
        down = [(j, i) for i, j in up]
        last = lax.slice_in_dim(value, length - width, length, axis=dim)
        first = lax.slice_in_dim(value, 0, width, axis=dim)
        before = lax.ppermute(last, axis, up)
        after = lax.ppermute(first, axis, down)
        value = jnp.concatenate([before, value, after], axis=dim)
    return value


def from_behind(block, axis, distance):
    devices = range(lax.axis_size(axis))
    route = [(i - distance, i) for i in devices if i - distance in devices]
    return lax.ppermute(block, axis, route)


def split_tables(length):
    indices = np.arange(length)
    angles = (indices[:, None] * indices[None, :] % length) * (2.0 * np.pi / length)
    cos_table = np.cos(angles) / np.sqrt(length)
    sin_table = np.sin(angles) / np.sqrt(length)
    forward = np.block([[cos_table, sin_table], [-sin_table, cos_table]])
    inverse = np.block([[cos_table, -sin_table], [sin_table, cos_table]])

    def halves(table):
        coarse = table.astype(np.float32).astype(ml_dtypes.bfloat16)
        fine = (table - coarse.astype(np.float64)).astype(ml_dtypes.bfloat16)
        return (coarse, fine)

    lefts, rights = ([], [])
    for left, right in ((forward, inverse), (inverse, forward)):
        coarse, fine = halves(left)
        lefts.append(np.concatenate([coarse, fine, coarse], axis=1))
        coarse, fine = halves(right)
        rights.append(np.concatenate([coarse, coarse, fine], axis=0))
    return (np.stack(lefts), np.stack(rights))


def halve(value):
    coarse = value.astype(jnp.bfloat16)
    return (coarse, (value - coarse.astype(jnp.float32)).astype(jnp.bfloat16))


def multiply(left, right):
    return jnp.dot(left, right, preferred_element_type=jnp.float32)


def from_left(table, value):
    coarse, fine = halve(value)
    return multiply(table, jnp.concatenate([coarse, coarse, fine], axis=0))


def from_right(value, table):
    coarse, fine = halve(value)
    return multiply(jnp.concatenate([coarse, fine, coarse], axis=1), table)


def regroup(value, length):
    top, bottom = (value[:length], value[length:])
    return jnp.concatenate(
        [
            jnp.concatenate([top[:, :length], bottom[:, :length]], axis=1),
            jnp.concatenate([top[:, length:], bottom[:, length:]], axis=1),
        ],
        axis=0,
    )


def slots_kernel(
    lead, starts, counts, object_map, probes, intensity, lefts, rights, totals, sums, window, far, lit
):
    modes, length = (probes.shape[1], probes.shape[-1])
    breadth = object_map.shape[-1]
    tall = length // 8
    per = modes // 2
    sublane = lax.broadcasted_iota(jnp.int32, (tall, 8, length), 1)
    sublane_more = lax.broadcasted_iota(jnp.int32, (tall + 1, 8, length), 1)
    totals[...] = jnp.zeros_like(totals)
    sums[...] = jnp.zeros_like(sums)
    lighting = jnp.zeros((length, length), jnp.float32)
    for mode in range(modes):
        lighting += probes[0, mode] * probes[0, mode] + probes[1, mode] * probes[1, mode]
    lit[...] = lighting

    def visit_slot(slot, carry):
        row, col = (starts[slot, 0], starts[slot, 1])
        tile = jnp.minimum(row // 8, object_map.shape[1] - tall - 1)
        shift = row - 8 * tile
        back = lax.rem(breadth + lead - col, breadth)
        onward = lax.rem(breadth - lead + col, breadth)
        for plane in range(2):
            wide = object_map[plane, pl.ds(tile, tall + 1)]
            wide = pltpu.roll(wide, back, 2)[:, :, :length]
            wide = pltpu.roll(wide, lax.rem(8 - shift, 8), 1)
            wide = jnp.where(sublane + shift < 8, wide[:tall], wide[1:])
            window[plane] = wide.reshape(length, length)
        modelled = jnp.zeros((length, length), jnp.float32)
        for pair in range(modes // 2):
            obj_r, obj_i = (window[0], window[1])
            waves_r, waves_i = ([], [])
            for mode in (2 * pair, 2 * pair + 1):
                waves_r.append(probes[0, mode] * obj_r - probes[1, mode] * obj_i)
                waves_i.append(probes[0, mode] * obj_i + probes[1, mode] * obj_r)
            wave = jnp.concatenate(
                [jnp.concatenate(waves_r, axis=1), jnp.concatenate(waves_i, axis=1)], axis=0
            )
            half = regroup(from_left(lefts[0], wave), length)
            spread = from_right(half, rights[0])
            far[pair] = spread
            power = spread * spread
            power = power[:, :length] + power[:, length:]
            modelled += power[:length] + power[length:]
        factor = jnp.sqrt(intensity[slot] / jnp.maximum(modelled, 1.0)) - 1.0
        factor = jnp.concatenate([factor, factor], axis=1)
        factor = jnp.concatenate([factor, factor], axis=0)
        terms_r = jnp.zeros((length, length), jnp.float32)
        terms_i = jnp.zeros((length, length), jnp.float32)
        for pair in range(modes // 2):
            half = regroup(from_right(far[pair] * factor, rights[1]), length)
            change = from_left(lefts[1], half)
            obj_r, obj_i = (window[0], window[1])
            for which in range(2):
                mode = 2 * pair + which
                lanes = slice(which * length, (which + 1) * length)
                change_r, change_i = (change[:length, lanes], change[length:, lanes])
                probe_r, probe_i = (probes[0, mode], probes[1, mode])
                terms_r += probe_r * change_r + probe_i * change_i
                terms_i += probe_r * change_i - probe_i * change_r
                stream, place = (mode // per, mode % per)
                sums[stream, place] += obj_r * change_r + obj_i * change_i
                sums[stream, per + place] += obj_r * change_i - obj_i * change_r
        coverage = window[0] * window[0] + window[1] * window[1]
        sums[0, 2 * per] += coverage
        sums[1, 2 * per] += coverage
        blank = jnp.zeros((1, 8, length), jnp.float32)
        margin = jnp.zeros((tall + 1, 8, breadth - length), jnp.float32)
        for plane, terms in enumerate((terms_r, terms_i, lit[...])):
            terms = pltpu.roll(terms.reshape(tall, 8, length), lax.rem(shift, 8), 1)
            terms = jnp.where(
                sublane_more >= shift,
                jnp.concatenate([terms, blank], axis=0),
                jnp.concatenate([blank, terms], axis=0),
            )
            wide = pltpu.roll(jnp.concatenate([terms, margin], axis=2), onward, 2)
            totals[plane, pl.ds(tile, tall + 1)] += wide
        return carry

    lax.fori_loop(0, counts[0], visit_slot, 0)


def accumulate(object_map, probes, starts, counts, intensity, lefts, rights, lead):
    _, modes, length, _ = probes.shape
    return pl.pallas_call(
        functools.partial(slots_kernel, lead),
        out_shape=(
            jax.ShapeDtypeStruct((3,) + object_map.shape[1:], jnp.float32),
            jax.ShapeDtypeStruct((2, modes + 1, length, length), jnp.float32),
        ),
        in_specs=[scalars, scalars] + [memory] * 5,
        out_specs=(memory, memory),
        scratch_shapes=[
            pltpu.VMEM((2, length, length), jnp.float32),
            pltpu.VMEM((modes // 2, 2 * length, 2 * length), jnp.float32),
            pltpu.VMEM((length, length), jnp.float32),
        ],
        compiler_params=pltpu.CompilerParams(vmem_limit_bytes=40 * 1024 * 1024),
        name="slots",
    )(starts, counts, object_map, probes, intensity, lefts, rights)


def mixing(probes, probe_step):
    mix_r = jnp.sum(probes[0] * probe_step[0] + probes[1] * probe_step[1], axis=0)
    mix_i = jnp.sum(probes[0] * probe_step[1] - probes[1] * probe_step[0], axis=0)
    return (mix_r, mix_i)


def cross_term(object_map, change, starts, active, mix_r, mix_i):
    length = mix_r.shape[-1]
    anchor_index = jnp.int32(0)

    def cross_visit_slot(running, element):
        corner_at, weight = element
        corner = (anchor_index, corner_at[0], corner_at[1])
        object_win = lax.dynamic_slice(object_map, corner, (2, length, length))
        change_win = lax.dynamic_slice(change, corner, (2, length, length))
        aligned = change_win[0] * object_win[0] + change_win[1] * object_win[1]
        rotated = change_win[0] * object_win[1] - change_win[1] * object_win[0]
        return (running + weight * jnp.sum(aligned * mix_r - rotated * mix_i), None)

    running, _ = lax.scan(cross_visit_slot, jnp.zeros((), jnp.float32), (starts, active))
    return running


def solve_steps(object_curve, cross_curve, probe_curve, object_slope, probe_slope):
    object_diag = 1.1 * object_curve + 0.001
    probe_diag = 1.1 * probe_curve + 0.001
    determinant = object_diag * probe_diag - cross_curve * cross_curve
    object_rate = (probe_diag * object_slope - cross_curve * probe_slope) / determinant
    probe_rate = (object_diag * probe_slope - cross_curve * object_slope) / determinant
    return (object_rate, probe_rate)


def widen(planes, margin):
    return with_halo(planes, (("tx", 1), ("ty", 2)), margin)


def fold_rims(totals, margin, height, breadth):
    middle = totals[:, margin : margin + height, :]
    for direction in (1, -1):
        border = totals[:, margin + height :, :] if direction == 1 else totals[:, :margin, :]
        arrived = from_behind(border, "tx", direction)
        if direction == 1:
            middle = jnp.concatenate([middle + arrived, middle[:, margin:, :]], axis=1)
        else:
            middle = jnp.concatenate([middle[:, : height - margin, :], middle + arrived], axis=1)
    interior = middle[:, :, margin : margin + breadth]
    for direction in (1, -1):
        border = middle[:, :, margin + breadth :] if direction == 1 else middle[:, :, :margin]
        arrived = from_behind(border, "ty", direction)
        if direction == 1:
            interior = jnp.concatenate(
                [interior[:, :, :margin] + arrived, interior[:, :, margin:]], axis=2
            )
        else:
            interior = jnp.concatenate(
                [interior[:, :, : breadth - margin], interior[:, :, breadth - margin :] + arrived],
                axis=2,
            )
    return interior


def general(object_field, probe_modes, positions, counts, intensity):
    length = probe_modes.shape[-1]
    margin = length // 2
    height = object_field.shape[1]
    breadth = object_field.shape[2]
    lefts, rights = split_tables(length)
    modes = probe_modes.shape[1]
    anchor = jnp.stack(
        [lax.axis_index("tx") * height - margin, lax.axis_index("ty") * breadth - margin]
    )
    starts = positions - anchor[None, :]
    active = (jnp.arange(positions.shape[0], dtype=jnp.int32) < counts[0]).astype(jnp.float32)
    object_map = object_field
    probes = probe_modes
    extended = widen(object_map, margin)
    for repeat in range(ITERS):
        tiled = extended.reshape(2, -1, 8, extended.shape[-1])
        totals, sums = accumulate(tiled, probes, starts, counts, intensity, lefts, rights, 0)
        totals = totals.reshape((3,) + extended.shape[1:])
        interior = fold_rims(totals, margin, height, breadth)
        change = interior[:2] / jnp.maximum(interior[2], 1.0)
        object_part = jnp.sum((change[0] * change[0] + change[1] * change[1]) * interior[2])
        slope_part = jnp.sum(interior[:2] * change)
        wide_change = widen(change, margin)
        sums = lax.psum(sums, ("tx", "ty"))
        probe_total = sums[:, :modes].reshape(2, 2, modes // 2, length, length)
        probe_total = jnp.swapaxes(probe_total, 0, 1).reshape(probes.shape)
        weight_total = sums[0, modes]
        probe_step = probe_total / (weight_total + 1e-05)
        mix_r, mix_i = mixing(probes, probe_step)
        cross_part = cross_term(extended, wide_change, starts, active, mix_r, mix_i)
        object_curve, cross_curve, object_slope = lax.psum(
            (object_part, cross_part, slope_part), ("tx", "ty")
        )
        probe_curve = jnp.sum(
            (probe_step[0] * probe_step[0] + probe_step[1] * probe_step[1]) * weight_total
        )
        probe_slope = jnp.sum(probe_total * probe_step)
        object_rate, probe_rate = solve_steps(
            object_curve, cross_curve, probe_curve, object_slope, probe_slope
        )
        object_map = object_map + object_rate * change
        probes = probes + probe_rate * probe_step
        if repeat + 1 < ITERS:
            extended = extended + object_rate * wide_change
    return (object_map, probes)


def greet(peers):
    barrier = pltpu.get_barrier_semaphore()
    for peer in peers:
        pl.semaphore_signal(barrier, 1, device_id=peer, device_id_type=pl.DeviceIdType.MESH)
    pl.semaphore_wait(barrier, len(peers))


def everyone(row, col):
    return [
        {"tx": (row + i) % 4, "ty": (col + j) % 4} for i in range(4) for j in range(4) if i or j
    ]


AROUND = [(i, j) for i in (-1, 0, 1) for j in (-1, 0, 1) if i or j]


def around(row, col, what):
    for k, (i, j) in enumerate(AROUND):
        inside = (row + i >= 0) & (row + i < 4) & (col + j >= 0) & (col + j < 4)
        pl.when(inside)(functools.partial(what, k, i, j))


def copy_to(source, target, send, arrive, index, peer):
    return pltpu.make_async_remote_copy(
        src_ref=source,
        dst_ref=target,
        send_sem=send.at[index],
        recv_sem=arrive.at[index],
        device_id=peer,
        device_id_type=pl.DeviceIdType.MESH,
    )


def halo_copy(block, halo, send, arrive, base, row, col, k, i, j):
    opposite = AROUND.index((-i, -j))
    return pltpu.make_async_remote_copy(
        src_ref=block,
        dst_ref=halo.at[opposite],
        send_sem=send.at[base + k],
        recv_sem=arrive.at[base + opposite],
        device_id={"tx": row + i, "ty": col + j},
        device_id_type=pl.DeviceIdType.MESH,
    )


def halo_wait(block, halo, send, arrive, base, row, col, k, i, j):
    halo_copy(block, halo, send, arrive, base, row, col, k, i, j).wait_send()
    pltpu.make_async_remote_copy(
        src_ref=block,
        dst_ref=halo.at[k],
        send_sem=send.at[base + k],
        recv_sem=arrive.at[base + k],
        device_id={"tx": row + i, "ty": col + j},
        device_id_type=pl.DeviceIdType.MESH,
    ).wait_recv()


def spread_halo(own, halo, wide):
    high, broad = (own.shape[1], own.shape[-1])
    early = lax.broadcasted_iota(jnp.int32, own.shape, 3) < broad // 2
    for i in (-1, 0, 1):
        rows = slice((i + 1) * high, (i + 2) * high)
        middle = own if i == 0 else halo[AROUND.index((i, 0))]
        wide[:, rows, :, :broad] = middle
        wide[:, rows, :, broad:] = jnp.where(
            early, halo[AROUND.index((i, 1))], halo[AROUND.index((i, -1))]
        )


def widen_kernel(own, wide, halo, send, arrive):
    row, col = (lax.axis_index("tx"), lax.axis_index("ty"))
    halo[...] = jnp.zeros_like(halo)
    greet(everyone(row, col))
    common = (own, halo, send, arrive, 0, row, col)
    around(row, col, lambda k, i, j: halo_copy(*common, k, i, j).start())
    around(row, col, lambda k, i, j: halo_wait(*common, k, i, j))
    spread_halo(own[...], halo, wide)


def widen_tiles(own):
    two, high, _, broad = own.shape
    return pl.pallas_call(
        widen_kernel,
        out_shape=jax.ShapeDtypeStruct((two, 3 * high, 8, 2 * broad), jnp.float32),
        in_specs=[memory],
        out_specs=memory,
        scratch_shapes=[
            pltpu.VMEM((8,) + own.shape, jnp.float32),
            pltpu.SemaphoreType.DMA((8,)),
            pltpu.SemaphoreType.DMA((8,)),
        ],
        compiler_params=pltpu.CompilerParams(
            collective_id=0, has_side_effects=True, vmem_limit_bytes=8 * 1024 * 1024
        ),
        cost_estimate=pl.CostEstimate(flops=0, bytes_accessed=30_000_000, transcendentals=0),
        name="widen",
    )(own)


def in_rows(values, lanes):
    at = lax.broadcasted_iota(jnp.int32, (8, lanes), 0)
    result = jnp.zeros((8, lanes), jnp.float32)
    for place, value in enumerate(values):
        result = jnp.where(at == place, value, result)
    return result


class Edges:
    def __init__(self, axis, source, target, base):
        self.axis, self.source, self.target, self.base = (axis, source, target, base)

    def each(self, what):
        here = lax.axis_index(self.axis)
        for k, ahead in ((0, -1), (1, 1)):
            peer = {"tx": lax.axis_index("tx"), "ty": lax.axis_index("ty")}
            peer[self.axis] = here + ahead
            pl.when((here + ahead >= 0) & (here + ahead < 4))(functools.partial(what, k, peer))

    def copy(self, k, landing, peer, send, arrive):
        return pltpu.make_async_remote_copy(
            src_ref=self.source(k),
            dst_ref=self.target(landing),
            send_sem=send.at[self.base + k],
            recv_sem=arrive.at[self.base + landing],
            device_id=peer,
            device_id_type=pl.DeviceIdType.MESH,
        )

    def start(self, send, arrive):
        self.each(lambda k, peer: self.copy(k, 1 - k, peer, send, arrive).start())

    def wait(self, send, arrive):
        def finish(k, peer):
            self.copy(k, 1 - k, peer, send, arrive).wait_send()
            self.copy(k, k, peer, send, arrive).wait_recv()

        self.each(finish)


def combine_kernel(
    totals, sums, wide, step, parts, beside, tall, over, column, near, r1, acc, ra2, acca, rb2, accb, ra3, rb3, got,
    send, arrive,
):
    row, col = (lax.axis_index("tx"), lax.axis_index("ty"))
    core, side = (col % 2, col // 2)
    planes = step.shape[1]
    high, broad = (over.shape[2], over.shape[-1])
    ends = (slice(0, high), slice(2 * high, 3 * high))
    middle = slice(high, 2 * high)
    for buffer in (beside, over, column, near):
        buffer[...] = jnp.zeros_like(buffer)
    greet(everyone(row, col))
    partner = {"tx": row, "ty": side * 2 + (1 - core)}
    across = {"tx": row, "ty": (1 - side) * 2 + core}
    along = [{"tx": (row + j) % 4, "ty": col} for j in (1, 2, 3)]

    first = copy_to(sums.at[:, :, pl.ds(8 * (1 - core), 8)], r1, send, arrive, 0, partner)
    first.start()

    broad_lanes = slice(broad, 2 * broad)
    fold_side = Edges("ty", lambda k: totals.at[:, :, :, broad_lanes], lambda k: beside.at[k], 24)
    fold_over = Edges("tx", lambda k: tall.at[:, ends[k]], lambda k: over.at[k], 26)
    halo_over = Edges("tx", lambda k: column.at[:, middle], lambda k: column.at[:, ends[k]], 28)
    halo_side = Edges("ty", lambda k: column, lambda k: near.at[k], 30)
    fold_side.start(send, arrive)

    first.wait()
    acc[...] = sums[:, :, pl.ds(8 * core, 8)] + r1[...]
    second = [copy_to(acc.at[0, :, pl.ds(4 * (1 - side), 4)], ra2, send, arrive, 1, across)]
    for j in (1, 2, 3):
        source = acc.at[1, :, pl.ds(2 * ((row + j) % 4), 2)]
        second.append(copy_to(source, rb2.at[j - 1], send, arrive, 1 + j, along[j - 1]))
    for copy in second:
        copy.start()

    fold_side.wait(send, arrive)
    early = lax.broadcasted_iota(jnp.int32, tall.shape, 3) < broad // 2
    tall[...] = totals[:, :, :, :broad] + jnp.where(early, beside[0], beside[1])
    fold_over.start(send, arrive)

    for copy in second:
        copy.wait()
    acca[...] = acc[0, :, pl.ds(4 * side, 4)] + ra2[...]
    accb[...] = acc[1, :, pl.ds(2 * row, 2)] + rb2[0] + rb2[1] + rb2[2]
    third = [copy_to(accb.at[:, pl.ds(1 - side, 1)], rb3, send, arrive, 5, across)]
    for j in (1, 2, 3):
        source = acca.at[:, pl.ds((row + j) % 4, 1)]
        third.append(copy_to(source, ra3.at[j - 1], send, arrive, 5 + j, along[j - 1]))
    for copy in third:
        copy.start()
    fold_over.wait(send, arrive)
    interior = tall[:, middle] + over[0] + over[1]
    change = interior[:2] / jnp.maximum(interior[2], 1.0)
    column[:, middle] = change
    halo_over.start(send, arrive)
    curve = jnp.sum((change[0] * change[0] + change[1] * change[1]) * interior[2])
    slope = jnp.sum(interior[:2] * change)
    for copy in third:
        copy.wait()
    sum_a = acca[:, pl.ds(row, 1)] + ra3[0] + ra3[1] + ra3[2]
    sum_b = accb[:, pl.ds(side, 1)] + rb3[...]
    at_a = 8 * core + 4 * side + row
    at_b = 8 * core + 2 * row + side
    probe_curve, probe_slope = (jnp.float32(0.0), jnp.float32(0.0))
    for stream, (total, at) in enumerate(((sum_a, at_a), (sum_b, at_b))):
        weight = total[planes:]
        found = total[:planes] / (weight + 1e-05)
        got[stream, :, pl.ds(at, 1)] = found
        probe_curve += jnp.sum(found * found * weight)
        probe_slope += jnp.sum(total[:planes] * found)

    def give(stream, at, count, index, peer):
        block = got.at[stream, :, pl.ds(at, count)]
        return copy_to(block, block, send, arrive, index, peer)

    fourth = [give(1, at_b, 1, 9, across)]
    for j in (1, 2, 3):
        fourth.append(give(0, at_a, 1, 9 + j, along[j - 1]))
    for copy in fourth:
        copy.start()
    halo_over.wait(send, arrive)
    halo_side.start(send, arrive)
    for copy in fourth:
        copy.wait()
    fifth = [give(0, 8 * core + 4 * side, 4, 13, across)]
    for j in (1, 2, 3):
        fifth.append(give(1, 8 * core + 2 * row, 2, 13 + j, along[j - 1]))
    for copy in fifth:
        copy.start()
    parts[...] = in_rows((curve, slope, probe_curve, probe_slope), parts.shape[-1])
    halo_side.wait(send, arrive)
    wide[:, :, :, :broad] = column[...]
    wide[:, :, :, broad:] = jnp.where(early[:2], near[1], near[0])
    for copy in fifth:
        copy.wait()
    block = got.at[:, :, pl.ds(8 * core, 8)]
    last = copy_to(block, block, send, arrive, 17, partner)
    last.start()
    last.wait()
    step[...] = got[...]


def combine(totals, sums):
    _, rows, _, lanes = totals.shape
    planes = sums.shape[1] - 1
    length = sums.shape[-1]
    high, broad = (rows // 3, lanes // 2)
    f32 = jnp.float32
    both = planes + 1
    return pl.pallas_call(
        combine_kernel,
        out_shape=(
            jax.ShapeDtypeStruct((2, rows, 8, lanes), f32),
            jax.ShapeDtypeStruct((2, planes, 16, 8, length), f32),
            jax.ShapeDtypeStruct((8, length), f32),
        ),
        in_specs=[memory] * 2,
        out_specs=(memory,) * 3,
        scratch_shapes=[
            pltpu.VMEM((2, 3, rows, 8, broad), f32),
            pltpu.VMEM((3, rows, 8, broad), f32),
            pltpu.VMEM((2, 3, high, 8, broad), f32),
            pltpu.VMEM((2, rows, 8, broad), f32),
            pltpu.VMEM((2, 2, rows, 8, broad), f32),
            pltpu.VMEM((2, both, 8, 8, length), f32),
            pltpu.VMEM((2, both, 8, 8, length), f32),
            pltpu.VMEM((both, 4, 8, length), f32),
            pltpu.VMEM((both, 4, 8, length), f32),
            pltpu.VMEM((3, both, 2, 8, length), f32),
            pltpu.VMEM((both, 2, 8, length), f32),
            pltpu.VMEM((3, both, 1, 8, length), f32),
            pltpu.VMEM((both, 1, 8, length), f32),
            pltpu.VMEM((2, planes, 16, 8, length), f32),
            pltpu.SemaphoreType.DMA((40,)),
            pltpu.SemaphoreType.DMA((40,)),
        ],
        compiler_params=pltpu.CompilerParams(
            collective_id=1, has_side_effects=True, vmem_limit_bytes=40 * 1024 * 1024
        ),
        name="combine",
    )(totals, sums.reshape(2, both, 16, 8, length))


def advance_kernel(
    places, weights, object_map, change, probes, step, parts, new_map, new_probes, product, held, mine,
    inbox, send, arrive,
):
    row, col = (lax.axis_index("tx"), lax.axis_index("ty"))
    peers = everyone(row, col)
    barrier = pltpu.get_barrier_semaphore()
    for peer in peers:
        pl.semaphore_signal(barrier, 1, device_id=peer, device_id_type=pl.DeviceIdType.MESH)
    length, modes = (probes.shape[-1], probes.shape[1])
    per, tall = (modes // 2, length // 8)
    product[0] = change[0] * object_map[0] + change[1] * object_map[1]
    product[1] = change[0] * object_map[1] - change[1] * object_map[0]
    held[...] = jnp.zeros_like(held)
    sublane = lax.broadcasted_iota(jnp.int32, (tall, 8, length), 1)

    def visit_slot(slot, carry):
        tile, back = (places[slot, 0], places[slot, 1])
        shift, upward, weight = (places[slot, 2], places[slot, 3], weights[slot])
        for plane in range(2):
            part = product[plane, pl.ds(tile, tall + 1)]
            part = pltpu.roll(part, back, 2)[:, :, :length]
            part = pltpu.roll(part, upward, 1)
            held[plane] += weight * jnp.where(sublane + shift < 8, part[:tall], part[1:])
        return carry

    lax.fori_loop(0, places.shape[0], visit_slot, 0)
    mix_r = jnp.zeros(held.shape[1:], jnp.float32)
    mix_i = jnp.zeros(held.shape[1:], jnp.float32)
    for mode in range(modes):
        stream, place = (mode // per, mode % per)
        step_r, step_i = (step[stream, place], step[stream, per + place])
        mix_r += probes[0, mode] * step_r + probes[1, mode] * step_i
        mix_i += probes[0, mode] * step_i - probes[1, mode] * step_r
    cross = jnp.sum(held[0] * mix_r - held[1] * mix_i)
    at = lax.broadcasted_iota(jnp.int32, parts.shape, 0)
    mine[...] = jnp.where(at == 4, cross, parts[...])
    pl.semaphore_wait(barrier, len(peers))
    copies = [copy_to(mine, inbox.at[k], send, arrive, k, peer) for k, peer in enumerate(peers)]
    for copy in copies:
        copy.start()
    for copy in copies:
        copy.wait()
    total = mine[...] + jnp.sum(inbox[...], axis=0)
    object_rate, probe_rate = solve_steps(
        total[0:1], total[4:5], total[2:3], total[1:2], total[3:4]
    )
    object_rate = jnp.broadcast_to(object_rate, (8, parts.shape[-1]))
    probe_rate = jnp.broadcast_to(probe_rate, (8, parts.shape[-1]))
    rates = jnp.concatenate([object_rate, object_rate], axis=1)
    new_map[...] = object_map[...] + rates * change[...]
    for mode in range(modes):
        stream, place = (mode // per, mode % per)
        new_probes[0, mode] = probes[0, mode] + probe_rate * step[stream, place]
        new_probes[1, mode] = probes[1, mode] + probe_rate * step[stream, per + place]


def advance(places, weights, object_map, change, probes, step, parts):
    return pl.pallas_call(
        advance_kernel,
        out_shape=(
            jax.ShapeDtypeStruct(object_map.shape, jnp.float32),
            jax.ShapeDtypeStruct(probes.shape, jnp.float32),
        ),
        in_specs=[scalars, scalars] + [memory] * 5,
        out_specs=(memory, memory),
        scratch_shapes=[
            pltpu.VMEM(object_map.shape, jnp.float32),
            pltpu.VMEM((2,) + probes.shape[2:], jnp.float32),
            pltpu.VMEM(parts.shape, jnp.float32),
            pltpu.VMEM((15,) + parts.shape, jnp.float32),
            pltpu.SemaphoreType.DMA((15,)),
            pltpu.SemaphoreType.DMA((15,)),
        ],
        compiler_params=pltpu.CompilerParams(
            collective_id=2, has_side_effects=True, vmem_limit_bytes=20 * 1024 * 1024
        ),
        name="advance",
    )(places, weights, object_map, change, probes, step, parts)


def direct(object_field, probe_modes, positions, counts, intensity):
    two, modes, length, _ = probe_modes.shape
    margin = length // 2
    _, height, breadth = object_field.shape
    lefts, rights = split_tables(length)
    anchor = jnp.stack(
        [lax.axis_index("tx") * height - margin, lax.axis_index("ty") * breadth - margin]
    )
    starts = positions - anchor[None, :]
    lanes = 2 * breadth
    rows_at = jnp.clip(starts[:, 0], 0, height + 2 * margin - length)
    cols_at = jnp.clip(starts[:, 1], 0, lanes - length)
    tile = jnp.minimum(rows_at // 8, (height + 2 * margin - length) // 8 - 1)
    shift = rows_at - 8 * tile
    back = (lanes + margin - cols_at) % lanes
    places = jnp.stack([tile, back, shift, (8 - shift) % 8], axis=1)
    weights = (jnp.arange(positions.shape[0], dtype=jnp.int32) < counts[0]).astype(jnp.float32)
    object_map = widen_tiles(object_field.reshape(2, height // 8, 8, breadth))
    probes = probe_modes
    for _ in range(ITERS):
        totals, sums = accumulate(
            object_map, probes, starts, counts, intensity, lefts, rights, margin
        )
        change, step, parts = combine(totals, sums)
        tiles = probes.reshape(2, modes, length // 8, 8, length)
        object_map, tiles = advance(places, weights, object_map, change, tiles, step, parts)
        probes = tiles.reshape(probes.shape)
    own = object_map[:, height // 8 : height // 4, :, :breadth]
    return (own.reshape(object_field.shape), probes)


def shards(object_field, probe_modes, positions, counts, intensity):
    _, height, breadth = object_field.shape
    length = probe_modes.shape[-1]
    grid = (lax.axis_size("tx"), lax.axis_size("ty"))
    arguments = (object_field, probe_modes, positions, counts, intensity)
    if grid == (4, 4) and length == 128 and (2 * height, breadth) == (length, length):
        return direct(*arguments)
    return general(*arguments)


def solution(mesh):
    return jax.shard_map(
        shards,
        mesh=mesh,
        in_specs=(
            P("groups", "tx", "ty"),
            P("groups", None, None, None),
            P(("groups", "tx", "ty"), None),
            P(("groups", "tx", "ty")),
            P(("groups", "tx", "ty"), None, None),
        ),
        out_specs=(P("groups", "tx", "ty"), P("groups", None, None, None)),
        check_vma=False,
    )
```

```python
import functools

import jax
import jax.numpy as jnp
import ml_dtypes
import numpy as np
from jax import lax
from jax.experimental import pallas as pl
from jax.experimental.pallas import tpu as pltpu
from jax.sharding import PartitionSpec as P

ITERS = 2
memory = pl.BlockSpec(memory_space=pltpu.VMEM)
scalars = pl.BlockSpec(memory_space=pltpu.SMEM)


def with_halo(value, sides, width):
    for axis, dim in sides:
        size, length = (lax.axis_size(axis), value.shape[dim])
        up = [(i, (i + 1) % size) for i in range(size - 1)]
        down = [(j, i) for i, j in up]
        last = lax.slice_in_dim(value, length - width, length, axis=dim)
        first = lax.slice_in_dim(value, 0, width, axis=dim)
        before = lax.ppermute(last, axis, up)
        after = lax.ppermute(first, axis, down)
        value = jnp.concatenate([before, value, after], axis=dim)
    return value


def from_behind(block, axis, distance):
    devices = range(lax.axis_size(axis))
    route = [(i - distance, i) for i in devices if i - distance in devices]
    return lax.ppermute(block, axis, route)


def split_tables(length):
    indices = np.arange(length)
    angles = (indices[:, None] * indices[None, :] % length) * (2.0 * np.pi / length)
    cos_table = np.cos(angles) / np.sqrt(length)
    sin_table = np.sin(angles) / np.sqrt(length)
    forward = np.block([[cos_table, sin_table], [-sin_table, cos_table]])
    inverse = np.block([[cos_table, -sin_table], [sin_table, cos_table]])

    def halves(table):
        coarse = table.astype(np.float32).astype(ml_dtypes.bfloat16)
        fine = (table - coarse.astype(np.float64)).astype(ml_dtypes.bfloat16)
        return (coarse, fine)

    return np.stack(halves(forward) + halves(inverse)).reshape(2, -1, 2 * length)


def halve(value):
    coarse = value.astype(jnp.bfloat16)
    return (coarse, (value - coarse.astype(jnp.float32)).astype(jnp.bfloat16))


def multiply(left, right):
    return jnp.dot(left, right, preferred_element_type=jnp.float32)


def from_left(table, value):
    coarse, fine = halve(value)
    both = multiply(table, coarse)
    size = value.shape[0]
    return both[:size] + both[size:] + multiply(table[:size], fine)


def from_right(value, table):
    coarse, fine = halve(value)
    size = value.shape[0]
    both = multiply(jnp.concatenate([coarse, fine], axis=0), table[: value.shape[1]])
    return both[:size] + both[size:] + multiply(coarse, table[value.shape[1] :])


def regroup(value, length):
    top, bottom = (value[:length], value[length:])
    return jnp.concatenate(
        [
            jnp.concatenate([top[:, :length], bottom[:, :length]], axis=1),
            jnp.concatenate([top[:, length:], bottom[:, length:]], axis=1),
        ],
        axis=0,
    )


def slots_kernel(
    lead, starts, counts, object_map, probes, intensity, turns, totals, sums, window, far, lit
):
    modes, length = (probes.shape[1], probes.shape[-1])
    breadth = object_map.shape[-1]
    tall = length // 8
    per = modes // 2
    sublane = lax.broadcasted_iota(jnp.int32, (tall, 8, length), 1)
    sublane_more = lax.broadcasted_iota(jnp.int32, (tall + 1, 8, length), 1)
    totals[...] = jnp.zeros_like(totals)
    sums[...] = jnp.zeros_like(sums)
    lighting = jnp.zeros((length, length), jnp.float32)
    for mode in range(modes):
        lighting += probes[0, mode] * probes[0, mode] + probes[1, mode] * probes[1, mode]
    lit[...] = lighting

    def visit_slot(slot, carry):
        row, col = (starts[slot, 0], starts[slot, 1])
        tile = jnp.minimum(row // 8, object_map.shape[1] - tall - 1)
        shift = row - 8 * tile
        back = lax.rem(breadth + lead - col, breadth)
        onward = lax.rem(breadth - lead + col, breadth)
        for plane in range(2):
            wide = object_map[plane, pl.ds(tile, tall + 1)]
            wide = pltpu.roll(wide, back, 2)[:, :, :length]
            wide = pltpu.roll(wide, lax.rem(8 - shift, 8), 1)
            wide = jnp.where(sublane + shift < 8, wide[:tall], wide[1:])
            window[plane] = wide.reshape(length, length)
        modelled = jnp.zeros((length, length), jnp.float32)
        for pair in range(modes // 2):
            obj_r, obj_i = (window[0], window[1])
            waves_r, waves_i = ([], [])
            for mode in (2 * pair, 2 * pair + 1):
                waves_r.append(probes[0, mode] * obj_r - probes[1, mode] * obj_i)
                waves_i.append(probes[0, mode] * obj_i + probes[1, mode] * obj_r)
            wave = jnp.concatenate(
                [jnp.concatenate(waves_r, axis=1), jnp.concatenate(waves_i, axis=1)], axis=0
            )
            half = regroup(from_left(turns[0], wave), length)
            spread = from_right(half, turns[1])
            far[pair] = spread
            power = spread * spread
            power = power[:, :length] + power[:, length:]
            modelled += power[:length] + power[length:]
        factor = jnp.sqrt(intensity[slot] / jnp.maximum(modelled, 1.0)) - 1.0
        factor = jnp.concatenate([factor, factor], axis=1)
        factor = jnp.concatenate([factor, factor], axis=0)
        terms_r = jnp.zeros((length, length), jnp.float32)
        terms_i = jnp.zeros((length, length), jnp.float32)
        for pair in range(modes // 2):
            half = regroup(from_right(far[pair] * factor, turns[0]), length)
            change = from_left(turns[1], half)
            obj_r, obj_i = (window[0], window[1])
            for which in range(2):
                mode = 2 * pair + which
                lanes = slice(which * length, (which + 1) * length)
                change_r, change_i = (change[:length, lanes], change[length:, lanes])
                probe_r, probe_i = (probes[0, mode], probes[1, mode])
                terms_r += probe_r * change_r + probe_i * change_i
                terms_i += probe_r * change_i - probe_i * change_r
                stream, place = (mode // per, mode % per)
                sums[stream, place] += obj_r * change_r + obj_i * change_i
                sums[stream, per + place] += obj_r * change_i - obj_i * change_r
        coverage = window[0] * window[0] + window[1] * window[1]
        sums[0, 2 * per] += coverage
        sums[1, 2 * per] += coverage
        blank = jnp.zeros((1, 8, length), jnp.float32)
        margin = jnp.zeros((tall + 1, 8, breadth - length), jnp.float32)
        for plane, terms in enumerate((terms_r, terms_i, lit[...])):
            terms = pltpu.roll(terms.reshape(tall, 8, length), lax.rem(shift, 8), 1)
            terms = jnp.where(
                sublane_more >= shift,
                jnp.concatenate([terms, blank], axis=0),
                jnp.concatenate([blank, terms], axis=0),
            )
            wide = pltpu.roll(jnp.concatenate([terms, margin], axis=2), onward, 2)
            totals[plane, pl.ds(tile, tall + 1)] += wide
        return carry

    lax.fori_loop(0, counts[0], visit_slot, 0)


def accumulate(object_map, probes, starts, counts, intensity, turns, lead):
    _, modes, length, _ = probes.shape
    return pl.pallas_call(
        functools.partial(slots_kernel, lead),
        out_shape=(
            jax.ShapeDtypeStruct((3,) + object_map.shape[1:], jnp.float32),
            jax.ShapeDtypeStruct((2, modes + 1, length, length), jnp.float32),
        ),
        in_specs=[scalars, scalars] + [memory] * 4,
        out_specs=(memory, memory),
        scratch_shapes=[
            pltpu.VMEM((2, length, length), jnp.float32),
            pltpu.VMEM((modes // 2, 2 * length, 2 * length), jnp.float32),
            pltpu.VMEM((length, length), jnp.float32),
        ],
        compiler_params=pltpu.CompilerParams(vmem_limit_bytes=40 * 1024 * 1024),
        name="slots",
    )(starts, counts, object_map, probes, intensity, turns)


def mixing(probes, probe_step):
    mix_r = jnp.sum(probes[0] * probe_step[0] + probes[1] * probe_step[1], axis=0)
    mix_i = jnp.sum(probes[0] * probe_step[1] - probes[1] * probe_step[0], axis=0)
    return (mix_r, mix_i)


def cross_term(object_map, change, starts, active, mix_r, mix_i):
    length = mix_r.shape[-1]
    anchor_index = jnp.int32(0)

    def cross_visit_slot(running, element):
        corner_at, weight = element
        corner = (anchor_index, corner_at[0], corner_at[1])
        object_win = lax.dynamic_slice(object_map, corner, (2, length, length))
        change_win = lax.dynamic_slice(change, corner, (2, length, length))
        aligned = change_win[0] * object_win[0] + change_win[1] * object_win[1]
        rotated = change_win[0] * object_win[1] - change_win[1] * object_win[0]
        return (running + weight * jnp.sum(aligned * mix_r - rotated * mix_i), None)

    running, _ = lax.scan(cross_visit_slot, jnp.zeros((), jnp.float32), (starts, active))
    return running


def solve_steps(object_curve, cross_curve, probe_curve, object_slope, probe_slope):
    object_diag = 1.1 * object_curve + 0.001
    probe_diag = 1.1 * probe_curve + 0.001
    determinant = object_diag * probe_diag - cross_curve * cross_curve
    object_rate = (probe_diag * object_slope - cross_curve * probe_slope) / determinant
    probe_rate = (object_diag * probe_slope - cross_curve * object_slope) / determinant
    return (object_rate, probe_rate)


def widen(planes, margin):
    return with_halo(planes, (("tx", 1), ("ty", 2)), margin)


def fold_rims(totals, margin, height, breadth):
    middle = totals[:, margin : margin + height, :]
    for direction in (1, -1):
        border = totals[:, margin + height :, :] if direction == 1 else totals[:, :margin, :]
        arrived = from_behind(border, "tx", direction)
        if direction == 1:
            middle = jnp.concatenate([middle + arrived, middle[:, margin:, :]], axis=1)
        else:
            middle = jnp.concatenate([middle[:, : height - margin, :], middle + arrived], axis=1)
    interior = middle[:, :, margin : margin + breadth]
    for direction in (1, -1):
        border = middle[:, :, margin + breadth :] if direction == 1 else middle[:, :, :margin]
        arrived = from_behind(border, "ty", direction)
        if direction == 1:
            interior = jnp.concatenate(
                [interior[:, :, :margin] + arrived, interior[:, :, margin:]], axis=2
            )
        else:
            interior = jnp.concatenate(
                [interior[:, :, : breadth - margin], interior[:, :, breadth - margin :] + arrived],
                axis=2,
            )
    return interior


def general(object_field, probe_modes, positions, counts, intensity):
    length = probe_modes.shape[-1]
    margin = length // 2
    height = object_field.shape[1]
    breadth = object_field.shape[2]
    turns = split_tables(length)
    modes = probe_modes.shape[1]
    anchor = jnp.stack(
        [lax.axis_index("tx") * height - margin, lax.axis_index("ty") * breadth - margin]
    )
    starts = positions - anchor[None, :]
    active = (jnp.arange(positions.shape[0], dtype=jnp.int32) < counts[0]).astype(jnp.float32)
    object_map = object_field
    probes = probe_modes
    extended = widen(object_map, margin)
    for repeat in range(ITERS):
        tiled = extended.reshape(2, -1, 8, extended.shape[-1])
        totals, sums = accumulate(tiled, probes, starts, counts, intensity, turns, 0)
        totals = totals.reshape((3,) + extended.shape[1:])
        interior = fold_rims(totals, margin, height, breadth)
        change = interior[:2] / jnp.maximum(interior[2], 1.0)
        object_part = jnp.sum((change[0] * change[0] + change[1] * change[1]) * interior[2])
        slope_part = jnp.sum(interior[:2] * change)
        wide_change = widen(change, margin)
        sums = lax.psum(sums, ("tx", "ty"))
        probe_total = sums[:, :modes].reshape(2, 2, modes // 2, length, length)
        probe_total = jnp.swapaxes(probe_total, 0, 1).reshape(probes.shape)
        weight_total = sums[0, modes]
        probe_step = probe_total / (weight_total + 1e-05)
        mix_r, mix_i = mixing(probes, probe_step)
        cross_part = cross_term(extended, wide_change, starts, active, mix_r, mix_i)
        object_curve, cross_curve, object_slope = lax.psum(
            (object_part, cross_part, slope_part), ("tx", "ty")
        )
        probe_curve = jnp.sum(
            (probe_step[0] * probe_step[0] + probe_step[1] * probe_step[1]) * weight_total
        )
        probe_slope = jnp.sum(probe_total * probe_step)
        object_rate, probe_rate = solve_steps(
            object_curve, cross_curve, probe_curve, object_slope, probe_slope
        )
        object_map = object_map + object_rate * change
        probes = probes + probe_rate * probe_step
        if repeat + 1 < ITERS:
            extended = extended + object_rate * wide_change
    return (object_map, probes)


def greet(peers):
    barrier = pltpu.get_barrier_semaphore()
    for peer in peers:
        pl.semaphore_signal(barrier, 1, device_id=peer, device_id_type=pl.DeviceIdType.MESH)
    pl.semaphore_wait(barrier, len(peers))


def everyone(row, col):
    return [
        {"tx": (row + i) % 4, "ty": (col + j) % 4} for i in range(4) for j in range(4) if i or j
    ]


AROUND = [(i, j) for i in (-1, 0, 1) for j in (-1, 0, 1) if i or j]


def around(row, col, what):
    for k, (i, j) in enumerate(AROUND):
        inside = (row + i >= 0) & (row + i < 4) & (col + j >= 0) & (col + j < 4)
        pl.when(inside)(functools.partial(what, k, i, j))


def copy_to(source, target, send, arrive, index, peer):
    return pltpu.make_async_remote_copy(
        src_ref=source,
        dst_ref=target,
        send_sem=send.at[index],
        recv_sem=arrive.at[index],
        device_id=peer,
        device_id_type=pl.DeviceIdType.MESH,
    )


def halo_copy(block, halo, send, arrive, base, row, col, k, i, j):
    opposite = AROUND.index((-i, -j))
    return pltpu.make_async_remote_copy(
        src_ref=block,
        dst_ref=halo.at[opposite],
        send_sem=send.at[base + k],
        recv_sem=arrive.at[base + opposite],
        device_id={"tx": row + i, "ty": col + j},
        device_id_type=pl.DeviceIdType.MESH,
    )


def halo_wait(block, halo, send, arrive, base, row, col, k, i, j):
    halo_copy(block, halo, send, arrive, base, row, col, k, i, j).wait_send()
    pltpu.make_async_remote_copy(
        src_ref=block,
        dst_ref=halo.at[k],
        send_sem=send.at[base + k],
        recv_sem=arrive.at[base + k],
        device_id={"tx": row + i, "ty": col + j},
        device_id_type=pl.DeviceIdType.MESH,
    ).wait_recv()


def spread_halo(own, halo, wide):
    high, broad = (own.shape[1], own.shape[-1])
    early = lax.broadcasted_iota(jnp.int32, own.shape, 3) < broad // 2
    for i in (-1, 0, 1):
        rows = slice((i + 1) * high, (i + 2) * high)
        middle = own if i == 0 else halo[AROUND.index((i, 0))]
        wide[:, rows, :, :broad] = middle
        wide[:, rows, :, broad:] = jnp.where(
            early, halo[AROUND.index((i, 1))], halo[AROUND.index((i, -1))]
        )


def widen_kernel(own, wide, halo, send, arrive):
    row, col = (lax.axis_index("tx"), lax.axis_index("ty"))
    halo[...] = jnp.zeros_like(halo)
    greet(everyone(row, col))
    common = (own, halo, send, arrive, 0, row, col)
    around(row, col, lambda k, i, j: halo_copy(*common, k, i, j).start())
    around(row, col, lambda k, i, j: halo_wait(*common, k, i, j))
    spread_halo(own[...], halo, wide)


def widen_tiles(own):
    two, high, _, broad = own.shape
    return pl.pallas_call(
        widen_kernel,
        out_shape=jax.ShapeDtypeStruct((two, 3 * high, 8, 2 * broad), jnp.float32),
        in_specs=[memory],
        out_specs=memory,
        scratch_shapes=[
            pltpu.VMEM((8,) + own.shape, jnp.float32),
            pltpu.SemaphoreType.DMA((8,)),
            pltpu.SemaphoreType.DMA((8,)),
        ],
        compiler_params=pltpu.CompilerParams(
            collective_id=0, has_side_effects=True, vmem_limit_bytes=8 * 1024 * 1024
        ),
        cost_estimate=pl.CostEstimate(flops=0, bytes_accessed=30_000_000, transcendentals=0),
        name="widen",
    )(own)


def in_rows(values, lanes):
    at = lax.broadcasted_iota(jnp.int32, (8, lanes), 0)
    result = jnp.zeros((8, lanes), jnp.float32)
    for place, value in enumerate(values):
        result = jnp.where(at == place, value, result)
    return result


class Edges:
    def __init__(self, axis, source, target, base):
        self.axis, self.source, self.target, self.base = (axis, source, target, base)

    def each(self, what):
        here = lax.axis_index(self.axis)
        for k, ahead in ((0, -1), (1, 1)):
            peer = {"tx": lax.axis_index("tx"), "ty": lax.axis_index("ty")}
            peer[self.axis] = here + ahead
            pl.when((here + ahead >= 0) & (here + ahead < 4))(functools.partial(what, k, peer))

    def copy(self, k, landing, peer, send, arrive):
        return pltpu.make_async_remote_copy(
            src_ref=self.source(k),
            dst_ref=self.target(landing),
            send_sem=send.at[self.base + k],
            recv_sem=arrive.at[self.base + landing],
            device_id=peer,
            device_id_type=pl.DeviceIdType.MESH,
        )

    def start(self, send, arrive):
        self.each(lambda k, peer: self.copy(k, 1 - k, peer, send, arrive).start())

    def wait(self, send, arrive):
        def finish(k, peer):
            self.copy(k, 1 - k, peer, send, arrive).wait_send()
            self.copy(k, k, peer, send, arrive).wait_recv()

        self.each(finish)


def combine_kernel(
    totals, sums, wide, step, parts, beside, tall, over, column, near, r1, acc, ra2, acca, rb2, accb, ra3, rb3, got,
    send, arrive,
):
    row, col = (lax.axis_index("tx"), lax.axis_index("ty"))
    core, side = (col % 2, col // 2)
    planes = step.shape[1]
    high, broad = (over.shape[2], over.shape[-1])
    ends = (slice(0, high), slice(2 * high, 3 * high))
    middle = slice(high, 2 * high)
    for buffer in (beside, over, column, near):
        buffer[...] = jnp.zeros_like(buffer)
    greet(everyone(row, col))
    partner = {"tx": row, "ty": side * 2 + (1 - core)}
    across = {"tx": row, "ty": (1 - side) * 2 + core}
    along = [{"tx": (row + j) % 4, "ty": col} for j in (1, 2, 3)]

    first = copy_to(sums.at[:, :, pl.ds(8 * (1 - core), 8)], r1, send, arrive, 0, partner)
    first.start()

    broad_lanes = slice(broad, 2 * broad)
    fold_side = Edges("ty", lambda k: totals.at[:, :, :, broad_lanes], lambda k: beside.at[k], 24)
    fold_over = Edges("tx", lambda k: tall.at[:, ends[k]], lambda k: over.at[k], 26)
    halo_over = Edges("tx", lambda k: column.at[:, middle], lambda k: column.at[:, ends[k]], 28)
    halo_side = Edges("ty", lambda k: column, lambda k: near.at[k], 30)
    fold_side.start(send, arrive)

    first.wait()
    acc[...] = sums[:, :, pl.ds(8 * core, 8)] + r1[...]
    second = [copy_to(acc.at[0, :, pl.ds(4 * (1 - side), 4)], ra2, send, arrive, 1, across)]
    for j in (1, 2, 3):
        source = acc.at[1, :, pl.ds(2 * ((row + j) % 4), 2)]
        second.append(copy_to(source, rb2.at[j - 1], send, arrive, 1 + j, along[j - 1]))
    for copy in second:
        copy.start()

    fold_side.wait(send, arrive)
    early = lax.broadcasted_iota(jnp.int32, tall.shape, 3) < broad // 2
    tall[...] = totals[:, :, :, :broad] + jnp.where(early, beside[0], beside[1])
    fold_over.start(send, arrive)

    for copy in second:
        copy.wait()
    acca[...] = acc[0, :, pl.ds(4 * side, 4)] + ra2[...]
    accb[...] = acc[1, :, pl.ds(2 * row, 2)] + rb2[0] + rb2[1] + rb2[2]
    third = [copy_to(accb.at[:, pl.ds(1 - side, 1)], rb3, send, arrive, 5, across)]
    for j in (1, 2, 3):
        source = acca.at[:, pl.ds((row + j) % 4, 1)]
        third.append(copy_to(source, ra3.at[j - 1], send, arrive, 5 + j, along[j - 1]))
    for copy in third:
        copy.start()
    fold_over.wait(send, arrive)
    interior = tall[:, middle] + over[0] + over[1]
    change = interior[:2] / jnp.maximum(interior[2], 1.0)
    column[:, middle] = change
    halo_over.start(send, arrive)
    curve = jnp.sum((change[0] * change[0] + change[1] * change[1]) * interior[2])
    slope = jnp.sum(interior[:2] * change)
    for copy in third:
        copy.wait()
    sum_a = acca[:, pl.ds(row, 1)] + ra3[0] + ra3[1] + ra3[2]
    sum_b = accb[:, pl.ds(side, 1)] + rb3[...]
    at_a = 8 * core + 4 * side + row
    at_b = 8 * core + 2 * row + side
    probe_curve, probe_slope = (jnp.float32(0.0), jnp.float32(0.0))
    for stream, (total, at) in enumerate(((sum_a, at_a), (sum_b, at_b))):
        weight = total[planes:]
        found = total[:planes] / (weight + 1e-05)
        got[stream, :, pl.ds(at, 1)] = found
        probe_curve += jnp.sum(found * found * weight)
        probe_slope += jnp.sum(total[:planes] * found)

    def give(stream, at, count, index, peer):
        block = got.at[stream, :, pl.ds(at, count)]
        return copy_to(block, block, send, arrive, index, peer)

    fourth = [give(1, at_b, 1, 9, across)]
    for j in (1, 2, 3):
        fourth.append(give(0, at_a, 1, 9 + j, along[j - 1]))
    for copy in fourth:
        copy.start()
    halo_over.wait(send, arrive)
    halo_side.start(send, arrive)
    for copy in fourth:
        copy.wait()
    fifth = [give(0, 8 * core + 4 * side, 4, 13, across)]
    for j in (1, 2, 3):
        fifth.append(give(1, 8 * core + 2 * row, 2, 13 + j, along[j - 1]))
    for copy in fifth:
        copy.start()
    parts[...] = in_rows((curve, slope, probe_curve, probe_slope), parts.shape[-1])
    halo_side.wait(send, arrive)
    wide[:, :, :, :broad] = column[...]
    wide[:, :, :, broad:] = jnp.where(early[:2], near[1], near[0])
    for copy in fifth:
        copy.wait()
    block = got.at[:, :, pl.ds(8 * core, 8)]
    last = copy_to(block, block, send, arrive, 17, partner)
    last.start()
    last.wait()
    step[...] = got[...]


def combine(totals, sums):
    _, rows, _, lanes = totals.shape
    planes = sums.shape[1] - 1
    length = sums.shape[-1]
    high, broad = (rows // 3, lanes // 2)
    f32 = jnp.float32
    both = planes + 1
    return pl.pallas_call(
        combine_kernel,
        out_shape=(
            jax.ShapeDtypeStruct((2, rows, 8, lanes), f32),
            jax.ShapeDtypeStruct((2, planes, 16, 8, length), f32),
            jax.ShapeDtypeStruct((8, length), f32),
        ),
        in_specs=[memory] * 2,
        out_specs=(memory,) * 3,
        scratch_shapes=[
            pltpu.VMEM((2, 3, rows, 8, broad), f32),
            pltpu.VMEM((3, rows, 8, broad), f32),
            pltpu.VMEM((2, 3, high, 8, broad), f32),
            pltpu.VMEM((2, rows, 8, broad), f32),
            pltpu.VMEM((2, 2, rows, 8, broad), f32),
            pltpu.VMEM((2, both, 8, 8, length), f32),
            pltpu.VMEM((2, both, 8, 8, length), f32),
            pltpu.VMEM((both, 4, 8, length), f32),
            pltpu.VMEM((both, 4, 8, length), f32),
            pltpu.VMEM((3, both, 2, 8, length), f32),
            pltpu.VMEM((both, 2, 8, length), f32),
            pltpu.VMEM((3, both, 1, 8, length), f32),
            pltpu.VMEM((both, 1, 8, length), f32),
            pltpu.VMEM((2, planes, 16, 8, length), f32),
            pltpu.SemaphoreType.DMA((40,)),
            pltpu.SemaphoreType.DMA((40,)),
        ],
        compiler_params=pltpu.CompilerParams(
            collective_id=1, has_side_effects=True, vmem_limit_bytes=40 * 1024 * 1024
        ),
        name="combine",
    )(totals, sums.reshape(2, both, 16, 8, length))


def advance_kernel(
    places, weights, object_map, change, probes, step, parts, new_map, new_probes, product, held, mine,
    inbox, send, arrive,
):
    row, col = (lax.axis_index("tx"), lax.axis_index("ty"))
    peers = everyone(row, col)
    barrier = pltpu.get_barrier_semaphore()
    for peer in peers:
        pl.semaphore_signal(barrier, 1, device_id=peer, device_id_type=pl.DeviceIdType.MESH)
    length, modes = (probes.shape[-1], probes.shape[1])
    per, tall = (modes // 2, length // 8)
    product[0] = change[0] * object_map[0] + change[1] * object_map[1]
    product[1] = change[0] * object_map[1] - change[1] * object_map[0]
    held[...] = jnp.zeros_like(held)
    sublane = lax.broadcasted_iota(jnp.int32, (tall, 8, length), 1)

    def visit_slot(slot, carry):
        tile, back = (places[slot, 0], places[slot, 1])
        shift, upward, weight = (places[slot, 2], places[slot, 3], weights[slot])
        for plane in range(2):
            part = product[plane, pl.ds(tile, tall + 1)]
            part = pltpu.roll(part, back, 2)[:, :, :length]
            part = pltpu.roll(part, upward, 1)
            held[plane] += weight * jnp.where(sublane + shift < 8, part[:tall], part[1:])
        return carry

    lax.fori_loop(0, places.shape[0], visit_slot, 0)
    mix_r = jnp.zeros(held.shape[1:], jnp.float32)
    mix_i = jnp.zeros(held.shape[1:], jnp.float32)
    for mode in range(modes):
        stream, place = (mode // per, mode % per)
        step_r, step_i = (step[stream, place], step[stream, per + place])
        mix_r += probes[0, mode] * step_r + probes[1, mode] * step_i
        mix_i += probes[0, mode] * step_i - probes[1, mode] * step_r
    cross = jnp.sum(held[0] * mix_r - held[1] * mix_i)
    at = lax.broadcasted_iota(jnp.int32, parts.shape, 0)
    mine[...] = jnp.where(at == 4, cross, parts[...])
    pl.semaphore_wait(barrier, len(peers))
    copies = [copy_to(mine, inbox.at[k], send, arrive, k, peer) for k, peer in enumerate(peers)]
    for copy in copies:
        copy.start()
    for copy in copies:
        copy.wait()
    total = mine[...] + jnp.sum(inbox[...], axis=0)
    object_rate, probe_rate = solve_steps(
        total[0:1], total[4:5], total[2:3], total[1:2], total[3:4]
    )
    object_rate = jnp.broadcast_to(object_rate, (8, parts.shape[-1]))
    probe_rate = jnp.broadcast_to(probe_rate, (8, parts.shape[-1]))
    rates = jnp.concatenate([object_rate, object_rate], axis=1)
    new_map[...] = object_map[...] + rates * change[...]
    for mode in range(modes):
        stream, place = (mode // per, mode % per)
        new_probes[0, mode] = probes[0, mode] + probe_rate * step[stream, place]
        new_probes[1, mode] = probes[1, mode] + probe_rate * step[stream, per + place]


def advance(places, weights, object_map, change, probes, step, parts):
    return pl.pallas_call(
        advance_kernel,
        out_shape=(
            jax.ShapeDtypeStruct(object_map.shape, jnp.float32),
            jax.ShapeDtypeStruct(probes.shape, jnp.float32),
        ),
        in_specs=[scalars, scalars] + [memory] * 5,
        out_specs=(memory, memory),
        scratch_shapes=[
            pltpu.VMEM(object_map.shape, jnp.float32),
            pltpu.VMEM((2,) + probes.shape[2:], jnp.float32),
            pltpu.VMEM(parts.shape, jnp.float32),
            pltpu.VMEM((15,) + parts.shape, jnp.float32),
            pltpu.SemaphoreType.DMA((15,)),
            pltpu.SemaphoreType.DMA((15,)),
        ],
        compiler_params=pltpu.CompilerParams(
            collective_id=2, has_side_effects=True, vmem_limit_bytes=20 * 1024 * 1024
        ),
        name="advance",
    )(places, weights, object_map, change, probes, step, parts)


def direct(object_field, probe_modes, positions, counts, intensity):
    two, modes, length, _ = probe_modes.shape
    margin = length // 2
    _, height, breadth = object_field.shape
    turns = split_tables(length)
    anchor = jnp.stack(
        [lax.axis_index("tx") * height - margin, lax.axis_index("ty") * breadth - margin]
    )
    starts = positions - anchor[None, :]
    lanes = 2 * breadth
    rows_at = jnp.clip(starts[:, 0], 0, height + 2 * margin - length)
    cols_at = jnp.clip(starts[:, 1], 0, lanes - length)
    tile = jnp.minimum(rows_at // 8, (height + 2 * margin - length) // 8 - 1)
    shift = rows_at - 8 * tile
    back = (lanes + margin - cols_at) % lanes
    places = jnp.stack([tile, back, shift, (8 - shift) % 8], axis=1)
    weights = (jnp.arange(positions.shape[0], dtype=jnp.int32) < counts[0]).astype(jnp.float32)
    object_map = widen_tiles(object_field.reshape(2, height // 8, 8, breadth))
    probes = probe_modes
    for _ in range(ITERS):
        totals, sums = accumulate(
            object_map, probes, starts, counts, intensity, turns, margin
        )
        change, step, parts = combine(totals, sums)
        tiles = probes.reshape(2, modes, length // 8, 8, length)
        object_map, tiles = advance(places, weights, object_map, change, tiles, step, parts)
        probes = tiles.reshape(probes.shape)
    own = object_map[:, height // 8 : height // 4, :, :breadth]
    return (own.reshape(object_field.shape), probes)


def shards(object_field, probe_modes, positions, counts, intensity):
    _, height, breadth = object_field.shape
    length = probe_modes.shape[-1]
    grid = (lax.axis_size("tx"), lax.axis_size("ty"))
    arguments = (object_field, probe_modes, positions, counts, intensity)
    if grid == (4, 4) and length == 128 and (2 * height, breadth) == (length, length):
        return direct(*arguments)
    return general(*arguments)


def solution(mesh):
    return jax.shard_map(
        shards,
        mesh=mesh,
        in_specs=(
            P("groups", "tx", "ty"),
            P("groups", None, None, None),
            P(("groups", "tx", "ty"), None),
            P(("groups", "tx", "ty")),
            P(("groups", "tx", "ty"), None, None),
        ),
        out_specs=(P("groups", "tx", "ty"), P("groups", None, None, None)),
        check_vma=False,
    )
```

```python
import functools

import jax
import jax.numpy as jnp
import ml_dtypes
import numpy as np
from jax import lax
from jax.experimental import pallas as pl
from jax.experimental.pallas import tpu as pltpu
from jax.sharding import PartitionSpec as P

ITERS = 2
memory = pl.BlockSpec(memory_space=pltpu.VMEM)
scalars = pl.BlockSpec(memory_space=pltpu.SMEM)


def with_halo(value, sides, width):
    for axis, dim in sides:
        size, length = (lax.axis_size(axis), value.shape[dim])
        up = [(i, (i + 1) % size) for i in range(size - 1)]
        down = [(j, i) for i, j in up]
        last = lax.slice_in_dim(value, length - width, length, axis=dim)
        first = lax.slice_in_dim(value, 0, width, axis=dim)
        before = lax.ppermute(last, axis, up)
        after = lax.ppermute(first, axis, down)
        value = jnp.concatenate([before, value, after], axis=dim)
    return value


def from_behind(block, axis, distance):
    devices = range(lax.axis_size(axis))
    route = [(i - distance, i) for i in devices if i - distance in devices]
    return lax.ppermute(block, axis, route)


def split_tables(length):
    indices = np.arange(length)
    angles = (indices[:, None] * indices[None, :] % length) * (2.0 * np.pi / length)
    cos_table = np.cos(angles) / np.sqrt(length)
    sin_table = np.sin(angles) / np.sqrt(length)
    forward = np.block([[cos_table, sin_table], [-sin_table, cos_table]])
    inverse = np.block([[cos_table, -sin_table], [sin_table, cos_table]])

    def halves(table):
        coarse = table.astype(np.float32).astype(ml_dtypes.bfloat16)
        fine = (table - coarse.astype(np.float64)).astype(ml_dtypes.bfloat16)
        return (coarse, fine)

    return np.stack(halves(forward) + halves(inverse)).reshape(2, -1, 2 * length)


def halve(value):
    coarse = value.astype(jnp.bfloat16)
    return (coarse, (value - coarse.astype(jnp.float32)).astype(jnp.bfloat16))


def multiply(left, right):
    return jnp.dot(left, right, preferred_element_type=jnp.float32)


def from_left(table, value):
    coarse, fine = halve(value)
    both = multiply(table, coarse)
    size = value.shape[0]
    return both[:size] + both[size:] + multiply(table[:size], fine)


def from_right(value, table):
    coarse, fine = halve(value)
    size = value.shape[0]
    both = multiply(jnp.concatenate([coarse, fine], axis=0), table[: value.shape[1]])
    return both[:size] + both[size:] + multiply(coarse, table[value.shape[1] :])


def regroup(value, length):
    top, bottom = (value[:length], value[length:])
    return jnp.concatenate(
        [
            jnp.concatenate([top[:, :length], bottom[:, :length]], axis=1),
            jnp.concatenate([top[:, length:], bottom[:, length:]], axis=1),
        ],
        axis=0,
    )


def slots_kernel(
    lead, starts, counts, object_map, probes, intensity, turns, totals, sums, window, far, lit
):
    modes, length = (probes.shape[1], probes.shape[-1])
    breadth = object_map.shape[-1]
    tall = length // 8
    per = modes // 2
    sublane = lax.broadcasted_iota(jnp.int32, (tall, 8, length), 1)
    sublane_more = lax.broadcasted_iota(jnp.int32, (tall + 1, 8, length), 1)
    totals[...] = jnp.zeros_like(totals)
    sums[...] = jnp.zeros_like(sums)
    lighting = jnp.zeros((length, length), jnp.float32)
    for mode in range(modes):
        lighting += probes[0, mode] * probes[0, mode] + probes[1, mode] * probes[1, mode]
    lit[...] = lighting

    def visit_slot(slot, carry):
        row, col = (starts[slot, 0], starts[slot, 1])
        tile = jnp.minimum(row // 8, object_map.shape[1] - tall - 1)
        shift = row - 8 * tile
        back = lax.rem(breadth + lead - col, breadth)
        onward = lax.rem(breadth - lead + col, breadth)
        for plane in range(2):
            wide = object_map[plane, pl.ds(tile, tall + 1)]
            wide = pltpu.roll(wide, back, 2)[:, :, :length]
            wide = pltpu.roll(wide, lax.rem(8 - shift, 8), 1)
            wide = jnp.where(sublane + shift < 8, wide[:tall], wide[1:])
            window[plane] = wide.reshape(length, length)
        modelled = jnp.zeros((length, length), jnp.float32)
        for pair in range(modes // 2):
            obj_r, obj_i = (window[0], window[1])
            waves_r, waves_i = ([], [])
            for mode in (2 * pair, 2 * pair + 1):
                waves_r.append(probes[0, mode] * obj_r - probes[1, mode] * obj_i)
                waves_i.append(probes[0, mode] * obj_i + probes[1, mode] * obj_r)
            wave = jnp.concatenate(
                [jnp.concatenate(waves_r, axis=1), jnp.concatenate(waves_i, axis=1)], axis=0
            )
            half = regroup(from_left(turns[0], wave), length)
            spread = from_right(half, turns[1])
            far[pair] = spread
            power = spread * spread
            power = power[:, :length] + power[:, length:]
            modelled += power[:length] + power[length:]
        factor = jnp.sqrt(intensity[slot] / jnp.maximum(modelled, 1.0)) - 1.0
        factor = jnp.concatenate([factor, factor], axis=1)
        factor = jnp.concatenate([factor, factor], axis=0)
        terms_r = jnp.zeros((length, length), jnp.float32)
        terms_i = jnp.zeros((length, length), jnp.float32)
        for pair in range(modes // 2):
            half = regroup(from_right(far[pair] * factor, turns[0]), length)
            change = from_left(turns[1], half)
            obj_r, obj_i = (window[0], window[1])
            for which in range(2):
                mode = 2 * pair + which
                lanes = slice(which * length, (which + 1) * length)
                change_r, change_i = (change[:length, lanes], change[length:, lanes])
                probe_r, probe_i = (probes[0, mode], probes[1, mode])
                terms_r += probe_r * change_r + probe_i * change_i
                terms_i += probe_r * change_i - probe_i * change_r
                stream, place = (mode // per, mode % per)
                sums[stream, place] += obj_r * change_r + obj_i * change_i
                sums[stream, per + place] += obj_r * change_i - obj_i * change_r
        coverage = window[0] * window[0] + window[1] * window[1]
        sums[0, 2 * per] += coverage
        sums[1, 2 * per] += coverage
        blank = jnp.zeros((1, 8, length), jnp.float32)
        margin = jnp.zeros((tall + 1, 8, breadth - length), jnp.float32)
        for plane, terms in enumerate((terms_r, terms_i, lit[...])):
            terms = pltpu.roll(terms.reshape(tall, 8, length), lax.rem(shift, 8), 1)
            terms = jnp.where(
                sublane_more >= shift,
                jnp.concatenate([terms, blank], axis=0),
                jnp.concatenate([blank, terms], axis=0),
            )
            wide = pltpu.roll(jnp.concatenate([terms, margin], axis=2), onward, 2)
            totals[plane, pl.ds(tile, tall + 1)] += wide
        return carry

    lax.fori_loop(0, counts[0], visit_slot, 0)


def accumulate(object_map, probes, starts, counts, intensity, turns, lead):
    _, modes, length, _ = probes.shape
    return pl.pallas_call(
        functools.partial(slots_kernel, lead),
        out_shape=(
            jax.ShapeDtypeStruct((3,) + object_map.shape[1:], jnp.float32),
            jax.ShapeDtypeStruct((2, modes + 1, length, length), jnp.float32),
        ),
        in_specs=[scalars, scalars] + [memory] * 4,
        out_specs=(memory, memory),
        scratch_shapes=[
            pltpu.VMEM((2, length, length), jnp.float32),
            pltpu.VMEM((modes // 2, 2 * length, 2 * length), jnp.float32),
            pltpu.VMEM((length, length), jnp.float32),
        ],
        compiler_params=pltpu.CompilerParams(vmem_limit_bytes=40 * 1024 * 1024),
        name="slots",
    )(starts, counts, object_map, probes, intensity, turns)


def mixing(probes, probe_step):
    mix_r = jnp.sum(probes[0] * probe_step[0] + probes[1] * probe_step[1], axis=0)
    mix_i = jnp.sum(probes[0] * probe_step[1] - probes[1] * probe_step[0], axis=0)
    return (mix_r, mix_i)


def cross_term(object_map, change, starts, active, mix_r, mix_i):
    length = mix_r.shape[-1]
    anchor_index = jnp.int32(0)

    def cross_visit_slot(running, element):
        corner_at, weight = element
        corner = (anchor_index, corner_at[0], corner_at[1])
        object_win = lax.dynamic_slice(object_map, corner, (2, length, length))
        change_win = lax.dynamic_slice(change, corner, (2, length, length))
        aligned = change_win[0] * object_win[0] + change_win[1] * object_win[1]
        rotated = change_win[0] * object_win[1] - change_win[1] * object_win[0]
        return (running + weight * jnp.sum(aligned * mix_r - rotated * mix_i), None)

    running, _ = lax.scan(cross_visit_slot, jnp.zeros((), jnp.float32), (starts, active))
    return running


def solve_steps(object_curve, cross_curve, probe_curve, object_slope, probe_slope):
    object_diag = 1.1 * object_curve + 0.001
    probe_diag = 1.1 * probe_curve + 0.001
    determinant = object_diag * probe_diag - cross_curve * cross_curve
    object_rate = (probe_diag * object_slope - cross_curve * probe_slope) / determinant
    probe_rate = (object_diag * probe_slope - cross_curve * object_slope) / determinant
    return (object_rate, probe_rate)


def widen(planes, margin):
    return with_halo(planes, (("tx", 1), ("ty", 2)), margin)


def fold_rims(totals, margin, height, breadth):
    middle = totals[:, margin : margin + height, :]
    for direction in (1, -1):
        border = totals[:, margin + height :, :] if direction == 1 else totals[:, :margin, :]
        arrived = from_behind(border, "tx", direction)
        if direction == 1:
            middle = jnp.concatenate([middle + arrived, middle[:, margin:, :]], axis=1)
        else:
            middle = jnp.concatenate([middle[:, : height - margin, :], middle + arrived], axis=1)
    interior = middle[:, :, margin : margin + breadth]
    for direction in (1, -1):
        border = middle[:, :, margin + breadth :] if direction == 1 else middle[:, :, :margin]
        arrived = from_behind(border, "ty", direction)
        if direction == 1:
            interior = jnp.concatenate(
                [interior[:, :, :margin] + arrived, interior[:, :, margin:]], axis=2
            )
        else:
            interior = jnp.concatenate(
                [interior[:, :, : breadth - margin], interior[:, :, breadth - margin :] + arrived],
                axis=2,
            )
    return interior


def general(object_field, probe_modes, positions, counts, intensity):
    length = probe_modes.shape[-1]
    margin = length // 2
    height = object_field.shape[1]
    breadth = object_field.shape[2]
    turns = split_tables(length)
    modes = probe_modes.shape[1]
    anchor = jnp.stack(
        [lax.axis_index("tx") * height - margin, lax.axis_index("ty") * breadth - margin]
    )
    starts = positions - anchor[None, :]
    active = (jnp.arange(positions.shape[0], dtype=jnp.int32) < counts[0]).astype(jnp.float32)
    object_map = object_field
    probes = probe_modes
    extended = widen(object_map, margin)
    for repeat in range(ITERS):
        tiled = extended.reshape(2, -1, 8, extended.shape[-1])
        totals, sums = accumulate(tiled, probes, starts, counts, intensity, turns, 0)
        totals = totals.reshape((3,) + extended.shape[1:])
        interior = fold_rims(totals, margin, height, breadth)
        change = interior[:2] / jnp.maximum(interior[2], 1.0)
        object_part = jnp.sum((change[0] * change[0] + change[1] * change[1]) * interior[2])
        slope_part = jnp.sum(interior[:2] * change)
        wide_change = widen(change, margin)
        sums = lax.psum(sums, ("tx", "ty"))
        probe_total = sums[:, :modes].reshape(2, 2, modes // 2, length, length)
        probe_total = jnp.swapaxes(probe_total, 0, 1).reshape(probes.shape)
        weight_total = sums[0, modes]
        probe_step = probe_total / (weight_total + 1e-05)
        mix_r, mix_i = mixing(probes, probe_step)
        cross_part = cross_term(extended, wide_change, starts, active, mix_r, mix_i)
        object_curve, cross_curve, object_slope = lax.psum(
            (object_part, cross_part, slope_part), ("tx", "ty")
        )
        probe_curve = jnp.sum(
            (probe_step[0] * probe_step[0] + probe_step[1] * probe_step[1]) * weight_total
        )
        probe_slope = jnp.sum(probe_total * probe_step)
        object_rate, probe_rate = solve_steps(
            object_curve, cross_curve, probe_curve, object_slope, probe_slope
        )
        object_map = object_map + object_rate * change
        probes = probes + probe_rate * probe_step
        if repeat + 1 < ITERS:
            extended = extended + object_rate * wide_change
    return (object_map, probes)


def greet(peers):
    barrier = pltpu.get_barrier_semaphore()
    for peer in peers:
        pl.semaphore_signal(barrier, 1, device_id=peer, device_id_type=pl.DeviceIdType.MESH)
    pl.semaphore_wait(barrier, len(peers))


def everyone(row, col):
    return [
        {"tx": (row + i) % 4, "ty": (col + j) % 4} for i in range(4) for j in range(4) if i or j
    ]


AROUND = [(i, j) for i in (-1, 0, 1) for j in (-1, 0, 1) if i or j]


def around(row, col, what):
    for k, (i, j) in enumerate(AROUND):
        inside = (row + i >= 0) & (row + i < 4) & (col + j >= 0) & (col + j < 4)
        pl.when(inside)(functools.partial(what, k, i, j))


def copy_to(source, target, send, arrive, index, peer):
    return pltpu.make_async_remote_copy(
        src_ref=source,
        dst_ref=target,
        send_sem=send.at[index],
        recv_sem=arrive.at[index],
        device_id=peer,
        device_id_type=pl.DeviceIdType.MESH,
    )


def halo_copy(block, halo, send, arrive, base, row, col, k, i, j):
    opposite = AROUND.index((-i, -j))
    return pltpu.make_async_remote_copy(
        src_ref=block,
        dst_ref=halo.at[opposite],
        send_sem=send.at[base + k],
        recv_sem=arrive.at[base + opposite],
        device_id={"tx": row + i, "ty": col + j},
        device_id_type=pl.DeviceIdType.MESH,
    )


def halo_wait(block, halo, send, arrive, base, row, col, k, i, j):
    halo_copy(block, halo, send, arrive, base, row, col, k, i, j).wait_send()
    pltpu.make_async_remote_copy(
        src_ref=block,
        dst_ref=halo.at[k],
        send_sem=send.at[base + k],
        recv_sem=arrive.at[base + k],
        device_id={"tx": row + i, "ty": col + j},
        device_id_type=pl.DeviceIdType.MESH,
    ).wait_recv()


def spread_halo(own, halo, wide):
    high, broad = (own.shape[1], own.shape[-1])
    early = lax.broadcasted_iota(jnp.int32, own.shape, 3) < broad // 2
    for i in (-1, 0, 1):
        rows = slice((i + 1) * high, (i + 2) * high)
        middle = own if i == 0 else halo[AROUND.index((i, 0))]
        wide[:, rows, :, :broad] = middle
        wide[:, rows, :, broad:] = jnp.where(
            early, halo[AROUND.index((i, 1))], halo[AROUND.index((i, -1))]
        )


def widen_kernel(own, wide, halo, send, arrive):
    row, col = (lax.axis_index("tx"), lax.axis_index("ty"))
    halo[...] = jnp.zeros_like(halo)
    greet(everyone(row, col))
    common = (own, halo, send, arrive, 0, row, col)
    around(row, col, lambda k, i, j: halo_copy(*common, k, i, j).start())
    around(row, col, lambda k, i, j: halo_wait(*common, k, i, j))
    spread_halo(own[...], halo, wide)


def widen_tiles(own):
    two, high, _, broad = own.shape
    return pl.pallas_call(
        widen_kernel,
        out_shape=jax.ShapeDtypeStruct((two, 3 * high, 8, 2 * broad), jnp.float32),
        in_specs=[memory],
        out_specs=memory,
        scratch_shapes=[
            pltpu.VMEM((8,) + own.shape, jnp.float32),
            pltpu.SemaphoreType.DMA((8,)),
            pltpu.SemaphoreType.DMA((8,)),
        ],
        compiler_params=pltpu.CompilerParams(
            collective_id=0, has_side_effects=True, vmem_limit_bytes=8 * 1024 * 1024
        ),
        cost_estimate=pl.CostEstimate(flops=0, bytes_accessed=30_000_000, transcendentals=0),
        name="widen",
    )(own)


def in_rows(values, lanes):
    at = lax.broadcasted_iota(jnp.int32, (8, lanes), 0)
    result = jnp.zeros((8, lanes), jnp.float32)
    for place, value in enumerate(values):
        result = jnp.where(at == place, value, result)
    return result


class Edges:
    def __init__(self, axis, source, target, base):
        self.axis, self.source, self.target, self.base = (axis, source, target, base)

    def each(self, what):
        here = lax.axis_index(self.axis)
        for k, ahead in ((0, -1), (1, 1)):
            peer = {"tx": lax.axis_index("tx"), "ty": lax.axis_index("ty")}
            peer[self.axis] = here + ahead
            pl.when((here + ahead >= 0) & (here + ahead < 4))(functools.partial(what, k, peer))

    def copy(self, k, landing, peer, send, arrive):
        return pltpu.make_async_remote_copy(
            src_ref=self.source(k),
            dst_ref=self.target(landing),
            send_sem=send.at[self.base + k],
            recv_sem=arrive.at[self.base + landing],
            device_id=peer,
            device_id_type=pl.DeviceIdType.MESH,
        )

    def start(self, send, arrive):
        self.each(lambda k, peer: self.copy(k, 1 - k, peer, send, arrive).start())

    def wait(self, send, arrive):
        def finish(k, peer):
            self.copy(k, 1 - k, peer, send, arrive).wait_send()
            self.copy(k, k, peer, send, arrive).wait_recv()

        self.each(finish)


def combine_kernel(
    totals, sums, wide, step, parts, beside, tall, over, column, near, r1, acc, ra2, acca, rb2, accb, ra3, rb3, got,
    send, arrive,
):
    row, col = (lax.axis_index("tx"), lax.axis_index("ty"))
    core, side = (col % 2, col // 2)
    planes = step.shape[1]
    high, broad = (over.shape[2], over.shape[-1])
    ends = (slice(0, high), slice(2 * high, 3 * high))
    middle = slice(high, 2 * high)
    for buffer in (beside, over, column, near):
        buffer[...] = jnp.zeros_like(buffer)
    greet(everyone(row, col))
    partner = {"tx": row, "ty": side * 2 + (1 - core)}
    across = {"tx": row, "ty": (1 - side) * 2 + core}
    along = [{"tx": (row + j) % 4, "ty": col} for j in (1, 2, 3)]

    first = copy_to(sums.at[:, :, pl.ds(8 * (1 - core), 8)], r1, send, arrive, 0, partner)
    first.start()

    broad_lanes = slice(broad, 2 * broad)
    fold_side = Edges("ty", lambda k: totals.at[:, :, :, broad_lanes], lambda k: beside.at[k], 24)
    fold_over = Edges("tx", lambda k: tall.at[:, ends[k]], lambda k: over.at[k], 26)
    halo_over = Edges("tx", lambda k: column.at[:, middle], lambda k: column.at[:, ends[k]], 28)
    halo_side = Edges("ty", lambda k: column, lambda k: near.at[k], 30)
    fold_side.start(send, arrive)

    first.wait()
    acc[...] = sums[:, :, pl.ds(8 * core, 8)] + r1[...]
    second = [copy_to(acc.at[0, :, pl.ds(4 * (1 - side), 4)], ra2, send, arrive, 1, across)]
    for j in (1, 2, 3):
        source = acc.at[1, :, pl.ds(2 * ((row + j) % 4), 2)]
        second.append(copy_to(source, rb2.at[j - 1], send, arrive, 1 + j, along[j - 1]))
    for copy in second:
        copy.start()

    fold_side.wait(send, arrive)
    early = lax.broadcasted_iota(jnp.int32, tall.shape, 3) < broad // 2
    tall[...] = totals[:, :, :, :broad] + jnp.where(early, beside[0], beside[1])
    fold_over.start(send, arrive)

    for copy in second:
        copy.wait()
    acca[...] = acc[0, :, pl.ds(4 * side, 4)] + ra2[...]
    accb[...] = acc[1, :, pl.ds(2 * row, 2)] + rb2[0] + rb2[1] + rb2[2]
    third = [copy_to(accb.at[:, pl.ds(1 - side, 1)], rb3, send, arrive, 5, across)]
    for j in (1, 2, 3):
        source = acca.at[:, pl.ds((row + j) % 4, 1)]
        third.append(copy_to(source, ra3.at[j - 1], send, arrive, 5 + j, along[j - 1]))
    for copy in third:
        copy.start()
    fold_over.wait(send, arrive)
    interior = tall[:, middle] + over[0] + over[1]
    change = interior[:2] / jnp.maximum(interior[2], 1.0)
    column[:, middle] = change
    halo_over.start(send, arrive)
    curve = jnp.sum((change[0] * change[0] + change[1] * change[1]) * interior[2])
    slope = jnp.sum(interior[:2] * change)
    for copy in third:
        copy.wait()
    sum_a = acca[:, pl.ds(row, 1)] + ra3[0] + ra3[1] + ra3[2]
    sum_b = accb[:, pl.ds(side, 1)] + rb3[...]
    at_a = 8 * core + 4 * side + row
    at_b = 8 * core + 2 * row + side
    probe_curve, probe_slope = (jnp.float32(0.0), jnp.float32(0.0))
    for stream, (total, at) in enumerate(((sum_a, at_a), (sum_b, at_b))):
        weight = total[planes:]
        found = total[:planes] / (weight + 1e-05)
        got[stream, :, pl.ds(at, 1)] = found
        probe_curve += jnp.sum(found * found * weight)
        probe_slope += jnp.sum(total[:planes] * found)

    def give(stream, at, count, index, peer):
        block = got.at[stream, :, pl.ds(at, count)]
        return copy_to(block, block, send, arrive, index, peer)

    fourth = [give(1, at_b, 1, 9, across)]
    for j in (1, 2, 3):
        fourth.append(give(0, at_a, 1, 9 + j, along[j - 1]))
    for copy in fourth:
        copy.start()
    halo_over.wait(send, arrive)
    halo_side.start(send, arrive)
    for copy in fourth:
        copy.wait()
    fifth = [give(0, 8 * core + 4 * side, 4, 13, across)]
    for j in (1, 2, 3):
        fifth.append(give(1, 8 * core + 2 * row, 2, 13 + j, along[j - 1]))
    for copy in fifth:
        copy.start()
    early_part = give(0, 8 * core + 4 * side, 4, 17, partner)
    early_part.start()
    parts[...] = in_rows((curve, slope, probe_curve, probe_slope), parts.shape[-1])
    halo_side.wait(send, arrive)
    wide[:, :, :, :broad] = column[...]
    wide[:, :, :, broad:] = jnp.where(early[:2], near[1], near[0])
    for copy in fifth:
        copy.wait()
    last = [
        give(0, 8 * core + 4 * (1 - side), 4, 18, partner),
        give(1, 8 * core, 8, 19, partner),
    ]
    for copy in last:
        copy.start()
    for copy in (early_part, *last):
        copy.wait()
    step[...] = got[...]


def combine(totals, sums):
    _, rows, _, lanes = totals.shape
    planes = sums.shape[1] - 1
    length = sums.shape[-1]
    high, broad = (rows // 3, lanes // 2)
    f32 = jnp.float32
    both = planes + 1
    return pl.pallas_call(
        combine_kernel,
        out_shape=(
            jax.ShapeDtypeStruct((2, rows, 8, lanes), f32),
            jax.ShapeDtypeStruct((2, planes, 16, 8, length), f32),
            jax.ShapeDtypeStruct((8, length), f32),
        ),
        in_specs=[memory] * 2,
        out_specs=(memory,) * 3,
        scratch_shapes=[
            pltpu.VMEM((2, 3, rows, 8, broad), f32),
            pltpu.VMEM((3, rows, 8, broad), f32),
            pltpu.VMEM((2, 3, high, 8, broad), f32),
            pltpu.VMEM((2, rows, 8, broad), f32),
            pltpu.VMEM((2, 2, rows, 8, broad), f32),
            pltpu.VMEM((2, both, 8, 8, length), f32),
            pltpu.VMEM((2, both, 8, 8, length), f32),
            pltpu.VMEM((both, 4, 8, length), f32),
            pltpu.VMEM((both, 4, 8, length), f32),
            pltpu.VMEM((3, both, 2, 8, length), f32),
            pltpu.VMEM((both, 2, 8, length), f32),
            pltpu.VMEM((3, both, 1, 8, length), f32),
            pltpu.VMEM((both, 1, 8, length), f32),
            pltpu.VMEM((2, planes, 16, 8, length), f32),
            pltpu.SemaphoreType.DMA((40,)),
            pltpu.SemaphoreType.DMA((40,)),
        ],
        compiler_params=pltpu.CompilerParams(
            collective_id=1, has_side_effects=True, vmem_limit_bytes=40 * 1024 * 1024
        ),
        name="combine",
    )(totals, sums.reshape(2, both, 16, 8, length))


def advance_kernel(
    places, weights, object_map, change, probes, step, parts, new_map, new_probes, product, held, mine,
    inbox, send, arrive,
):
    row, col = (lax.axis_index("tx"), lax.axis_index("ty"))
    peers = everyone(row, col)
    barrier = pltpu.get_barrier_semaphore()
    for peer in peers:
        pl.semaphore_signal(barrier, 1, device_id=peer, device_id_type=pl.DeviceIdType.MESH)
    length, modes = (probes.shape[-1], probes.shape[1])
    per, tall = (modes // 2, length // 8)
    product[0] = change[0] * object_map[0] + change[1] * object_map[1]
    product[1] = change[0] * object_map[1] - change[1] * object_map[0]
    held[...] = jnp.zeros_like(held)
    sublane = lax.broadcasted_iota(jnp.int32, (tall, 8, length), 1)

    def visit_slot(slot, carry):
        tile, back = (places[slot, 0], places[slot, 1])
        shift, upward, weight = (places[slot, 2], places[slot, 3], weights[slot])
        for plane in range(2):
            part = product[plane, pl.ds(tile, tall + 1)]
            part = pltpu.roll(part, back, 2)[:, :, :length]
            part = pltpu.roll(part, upward, 1)
            held[plane] += weight * jnp.where(sublane + shift < 8, part[:tall], part[1:])
        return carry

    lax.fori_loop(0, places.shape[0], visit_slot, 0)
    mix_r = jnp.zeros(held.shape[1:], jnp.float32)
    mix_i = jnp.zeros(held.shape[1:], jnp.float32)
    for mode in range(modes):
        stream, place = (mode // per, mode % per)
        step_r, step_i = (step[stream, place], step[stream, per + place])
        mix_r += probes[0, mode] * step_r + probes[1, mode] * step_i
        mix_i += probes[0, mode] * step_i - probes[1, mode] * step_r
    cross = jnp.sum(held[0] * mix_r - held[1] * mix_i)
    at = lax.broadcasted_iota(jnp.int32, parts.shape, 0)
    mine[...] = jnp.where(at == 4, cross, parts[...])
    pl.semaphore_wait(barrier, len(peers))
    copies = [copy_to(mine, inbox.at[k], send, arrive, k, peer) for k, peer in enumerate(peers)]
    for copy in copies:
        copy.start()
    for copy in copies:
        copy.wait()
    total = mine[...] + jnp.sum(inbox[...], axis=0)
    object_rate, probe_rate = solve_steps(
        total[0:1], total[4:5], total[2:3], total[1:2], total[3:4]
    )
    object_rate = jnp.broadcast_to(object_rate, (8, parts.shape[-1]))
    probe_rate = jnp.broadcast_to(probe_rate, (8, parts.shape[-1]))
    rates = jnp.concatenate([object_rate, object_rate], axis=1)
    new_map[...] = object_map[...] + rates * change[...]
    for mode in range(modes):
        stream, place = (mode // per, mode % per)
        new_probes[0, mode] = probes[0, mode] + probe_rate * step[stream, place]
        new_probes[1, mode] = probes[1, mode] + probe_rate * step[stream, per + place]


def advance(places, weights, object_map, change, probes, step, parts):
    return pl.pallas_call(
        advance_kernel,
        out_shape=(
            jax.ShapeDtypeStruct(object_map.shape, jnp.float32),
            jax.ShapeDtypeStruct(probes.shape, jnp.float32),
        ),
        in_specs=[scalars, scalars] + [memory] * 5,
        out_specs=(memory, memory),
        scratch_shapes=[
            pltpu.VMEM(object_map.shape, jnp.float32),
            pltpu.VMEM((2,) + probes.shape[2:], jnp.float32),
            pltpu.VMEM(parts.shape, jnp.float32),
            pltpu.VMEM((15,) + parts.shape, jnp.float32),
            pltpu.SemaphoreType.DMA((15,)),
            pltpu.SemaphoreType.DMA((15,)),
        ],
        compiler_params=pltpu.CompilerParams(
            collective_id=2, has_side_effects=True, vmem_limit_bytes=20 * 1024 * 1024
        ),
        name="advance",
    )(places, weights, object_map, change, probes, step, parts)


def direct(object_field, probe_modes, positions, counts, intensity):
    two, modes, length, _ = probe_modes.shape
    margin = length // 2
    _, height, breadth = object_field.shape
    turns = split_tables(length)
    anchor = jnp.stack(
        [lax.axis_index("tx") * height - margin, lax.axis_index("ty") * breadth - margin]
    )
    starts = positions - anchor[None, :]
    lanes = 2 * breadth
    rows_at = jnp.clip(starts[:, 0], 0, height + 2 * margin - length)
    cols_at = jnp.clip(starts[:, 1], 0, lanes - length)
    tile = jnp.minimum(rows_at // 8, (height + 2 * margin - length) // 8 - 1)
    shift = rows_at - 8 * tile
    back = (lanes + margin - cols_at) % lanes
    places = jnp.stack([tile, back, shift, (8 - shift) % 8], axis=1)
    weights = (jnp.arange(positions.shape[0], dtype=jnp.int32) < counts[0]).astype(jnp.float32)
    object_map = widen_tiles(object_field.reshape(2, height // 8, 8, breadth))
    probes = probe_modes
    for _ in range(ITERS):
        totals, sums = accumulate(
            object_map, probes, starts, counts, intensity, turns, margin
        )
        change, step, parts = combine(totals, sums)
        tiles = probes.reshape(2, modes, length // 8, 8, length)
        object_map, tiles = advance(places, weights, object_map, change, tiles, step, parts)
        probes = tiles.reshape(probes.shape)
    own = object_map[:, height // 8 : height // 4, :, :breadth]
    return (own.reshape(object_field.shape), probes)


def shards(object_field, probe_modes, positions, counts, intensity):
    _, height, breadth = object_field.shape
    length = probe_modes.shape[-1]
    grid = (lax.axis_size("tx"), lax.axis_size("ty"))
    arguments = (object_field, probe_modes, positions, counts, intensity)
    if grid == (4, 4) and length == 128 and (2 * height, breadth) == (length, length):
        return direct(*arguments)
    return general(*arguments)


def solution(mesh):
    return jax.shard_map(
        shards,
        mesh=mesh,
        in_specs=(
            P("groups", "tx", "ty"),
            P("groups", None, None, None),
            P(("groups", "tx", "ty"), None),
            P(("groups", "tx", "ty")),
            P(("groups", "tx", "ty"), None, None),
        ),
        out_specs=(P("groups", "tx", "ty"), P("groups", None, None, None)),
        check_vma=False,
    )
```
